32 devices in a mesh: sx: 8 (over z, x), sy: 4 (over y, core).
Axes of the slice: x: 2, y: 2, z: 4, core: 2. Of those that a mesh axis runs over, the one named last changes fastest.
Arguments:
- charges: bfloat16 [2048, 64, 128], P(('sx', 'sy')), may hold values from -6 to 6
- near_blocks: bfloat16 [2048, 6, 128, 128], P(('sx', 'sy')), may hold values from -0.21875 to 0.21875
- near_list: int32 [2048, 6], P(('sx', 'sy')), may hold values from 0 to 2047, as said below
- leaf_basis: bfloat16 [2048, 64, 128], P(('sx', 'sy')), may hold values from -0.5 to 0.5
- child_transfer: bfloat16 [2048, 64, 64], P(('sx', 'sy')), may hold values from -0.5 to 0.5
- parent_transfer: bfloat16 [256, 64, 64], P(('sx', 'sy')), may hold values from -0.5 to 0.5
- m2l_ops: bfloat16 [2, 316, 64, 64], replicated, may hold values from -0.15625 to 0.15625
- far_list0: int32 [2048, 24], P(('sx', 'sy')), may hold values from 0 to 2047, as said below
- far_op0: int32 [2048, 24], P(('sx', 'sy')), may hold values from 0 to 315
- far_list1: int32 [256, 24], P(('sx', 'sy')), may hold values from 0 to 255, as said below
- far_op1: int32 [256, 24], P(('sx', 'sy')), may hold values from 0 to 315
- top_transfer: float32 [64, 64], replicated, may hold values from -0.5 to 0.5
- top_couple: float32 [64, 64], replicated, may hold values from -0.75 to 0.75
Outputs:
- product: float32 [2048, 64, 128], P(('sx', 'sy'))
The draws below stay inside these ranges and needn't reach their ends.
Inputs may be any that keep to these rules, and one draw needn't show every extreme that they name: `near_list`: each entry is a leaf id whose distance from its own row's leaf id is at most 64; entry 0 is the row's own leaf; the distance 64 is taken. `far_list0`: each entry is a leaf id whose distance from its own row's leaf id is at most 64; the distance 64 is taken. `far_list1`: each entry is a parent id whose distance from its own row's parent id is at most 8; the distance 8 is taken.
All inputs are finite; a program needn't handle non-finite values.
Results may differ from the reference program's by a relative error of at most 0.008.
Values may be sent and summed in bfloat16 or wider, within the bound.
No kernel may reach another device: no remote copies, remote signals or barrier semaphores. Data moves between devices by JAX's collectives and lax.ppermute only.
A program may use at most 192 MiB of HBM per device.

```python
import jax
import jax.numpy as jnp
from jax import lax

P_SIZE = 128
K = 64
R = 64
NEAR = 6
FAR0 = 24
FAR1 = 24
OPS = 316
LEAVES = 2048
PARENTS = 256
BOXES = 32
LEAF_RIM = 64
PARENT_RIM = 8


def window_ids(key, rowcount, columns, reach, with_self):
    offsets = jax.random.randint(key, (rowcount, columns), -reach, reach + 1)
    rows = jnp.arange(rowcount, dtype=jnp.int32)[:, None]
    places = jnp.arange(columns, dtype=jnp.int32)[None, :]
    extreme = jnp.where(rows % 8 == 0, -reach, reach)
    offsets = jnp.where((places == 1) & (rows % 4 == 0), extreme, offsets)
    if with_self:
        offsets = jnp.where(places == 0, 0, offsets)
    return jnp.clip(rows + offsets, 0, rowcount - 1).astype(jnp.int32)


def draw_near_list(key, part):
    return window_ids(jax.random.fold_in(key, 11), LEAVES, NEAR, LEAF_RIM, True)


def draw_far_list0(key, part):
    return window_ids(jax.random.fold_in(key, 23), LEAVES, FAR0, LEAF_RIM, False)


def draw_far_list1(key, part):
    return window_ids(jax.random.fold_in(key, 37), PARENTS, FAR1, PARENT_RIM, False)


def with_ends(values, key, smallest, top_value):
    index_at = [jax.random.randint(jax.random.fold_in(key, axis), (), 0, length) for axis, length in enumerate(values.shape)]
    longest = values.shape.index(max(values.shape))
    next_to = index_at[:longest] + [(index_at[longest] + 1) % values.shape[longest]] + index_at[longest + 1:]
    return values.at[tuple(index_at)].set(smallest).at[tuple(next_to)].set(top_value)


def levels(key, extent, shards, low, high):
    factor_of = 1.0
    for position, parts in shards:
        heights = jax.random.uniform(jax.random.fold_in(jax.random.fold_in(key, 6), position), (parts,), jnp.float32, low / len(shards), high / len(shards))
        factor_of = factor_of * jnp.repeat(jnp.exp(heights), extent[position] // parts).reshape((-1,) + (1,) * (len(extent) - 1 - position))
    return factor_of


def noise(stream_key, extent, scale, most, cuts=(), kind=jnp.bfloat16):
    factor_of = levels(stream_key, extent, cuts, -0.22, 0.18) if cuts else 1.0
    drawn = jax.random.normal(stream_key, extent, jnp.float32) * scale * factor_of
    return jnp.minimum(jnp.maximum(drawn, -most), most).astype(kind)


def setup_inputs(seed: int = 0) -> dict:
    key_of = jax.random.split(jax.random.key(seed), 14)
    charges = noise(key_of[0], (LEAVES, R, P_SIZE), 1.0, 6.0, ((0, 32),))
    near_blocks = noise(key_of[1], (LEAVES, NEAR, P_SIZE, P_SIZE), (NEAR * P_SIZE) ** -0.5, 0.21875, ((0, 32),))
    near_list = draw_near_list(jax.random.fold_in(key_of[13], 71), 0)
    leaf_basis = noise(key_of[3], (LEAVES, K, P_SIZE), P_SIZE ** -0.5, 0.5, ((0, 32),))
    child_transfer = noise(key_of[4], (LEAVES, K, K), (2 * K) ** -0.5, 0.5, ((0, 32),))
    parent_transfer = noise(key_of[5], (PARENTS, K, K), (2 * K) ** -0.5, 0.5, ((0, 32),))
    m2l_ops = noise(key_of[6], (2, OPS, K, K), (K * FAR0) ** -0.5, 0.15625)
    far_list0 = draw_far_list0(jax.random.fold_in(key_of[13], 71), 0)
    far_op0 = with_ends(jax.random.randint(key_of[8], (LEAVES, FAR0), 0, OPS), jax.random.fold_in(key_of[8], 1), 0, OPS - 1).astype(jnp.int32)
    far_list1 = draw_far_list1(jax.random.fold_in(key_of[13], 71), 0)
    far_op1 = with_ends(jax.random.randint(key_of[10], (PARENTS, FAR1), 0, OPS), jax.random.fold_in(key_of[10], 1), 0, OPS - 1).astype(jnp.int32)
    top_transfer = noise(key_of[11], (K, K), (2 * K) ** -0.5, 0.5, (), jnp.float32)
    top_couple = noise(key_of[12], (K, K), K ** -0.5, 0.75, (), jnp.float32)
    return dict(charges=charges, near_blocks=near_blocks, near_list=near_list, leaf_basis=leaf_basis, child_transfer=child_transfer, parent_transfer=parent_transfer, m2l_ops=m2l_ops, far_list0=far_list0, far_op0=far_op0, far_list1=far_list1, far_op1=far_op1, top_transfer=top_transfer, top_couple=top_couple)


highest = lax.Precision.HIGHEST


def translate(moments, sources, op_ids, table):
    def advance(running, column):
        picked = jnp.take(moments, jnp.take(sources, column, axis=1), axis=0).astype(jnp.float32)
        matrices = jnp.take(table, jnp.take(op_ids, column, axis=1), axis=0).astype(jnp.float32)
        return running + jnp.einsum('nrk,nkj->nrj', picked, matrices, precision=highest), None
    starting = jnp.zeros((sources.shape[0], moments.shape[1], table.shape[2]), jnp.float32)
    running, unused = lax.scan(advance, starting, jnp.arange(sources.shape[1]))
    return running


def top_tree(box_moments, top_transfer, top_couple):
    height = box_moments.shape[0].bit_length() - 1
    siblings = []
    current = box_moments
    for level_bit in range(height):
        amount = current.shape[0]
        paired = current.reshape(amount // 2, 2, current.shape[1], current.shape[2])
        siblings.append(paired[:, ::-1].reshape(current.shape))
        if level_bit + 1 < height:
            current = jnp.einsum('nrk,kj->nrj', paired[:, 0] + paired[:, 1], top_transfer, precision=highest)
    downward = jnp.zeros((1, box_moments.shape[1], box_moments.shape[2]), jnp.float32)
    for level_bit in reversed(range(height)):
        downward = jnp.repeat(downward, 2, axis=0)
        downward = jnp.einsum('nrj,kj->nrk', downward, top_transfer, precision=highest) + jnp.einsum('nrk,kj->nrj', siblings[level_bit], top_couple, precision=highest)
    return downward


def reference(charges, near_blocks, near_list, leaf_basis, child_transfer, parent_transfer, m2l_ops, far_list0, far_op0, far_list1, far_op1, top_transfer, top_couple):
    moments = jnp.einsum('lrp,lkp->lrk', charges.astype(jnp.float32), leaf_basis.astype(jnp.float32), precision=highest).astype(jnp.bfloat16)
    child_groups = child_transfer.astype(jnp.float32).reshape(PARENTS, 8, K, K)
    parent_moments = jnp.einsum('pcrk,pckj->prj', moments.astype(jnp.float32).reshape(PARENTS, 8, R, K), child_groups, precision=highest).astype(jnp.bfloat16)
    parent_groups = parent_transfer.astype(jnp.float32).reshape(BOXES, 8, K, K)
    box_moments = jnp.einsum('bcrk,bckj->brj', parent_moments.astype(jnp.float32).reshape(BOXES, 8, R, K), parent_groups, precision=highest)
    box_locals = top_tree(box_moments, top_transfer, top_couple).astype(jnp.bfloat16)
    parent_locals = jnp.einsum('brj,bckj->bcrk', box_locals.astype(jnp.float32), parent_groups, precision=highest).reshape(PARENTS, R, K)
    parent_locals = (parent_locals + translate(parent_moments, far_list1, far_op1, m2l_ops[1])).astype(jnp.bfloat16)
    leaf_locals = jnp.einsum('prj,pckj->pcrk', parent_locals.astype(jnp.float32), child_groups, precision=highest).reshape(LEAVES, R, K)
    leaf_locals = (leaf_locals + translate(moments, far_list0, far_op0, m2l_ops[0])).astype(jnp.bfloat16)
    far_part = jnp.einsum('lrk,lkp->lrp', leaf_locals.astype(jnp.float32), leaf_basis.astype(jnp.float32), precision=highest)

    def near_step(running, column):
        picked = jnp.take(charges, jnp.take(near_list, column, axis=1), axis=0).astype(jnp.float32)
        blocks = jnp.take(near_blocks, column, axis=1).astype(jnp.float32)
        return running + jnp.einsum('lrq,lpq->lrp', picked, blocks, precision=highest), None

    near_part, unused = lax.scan(near_step, jnp.zeros((LEAVES, R, P_SIZE), jnp.float32), jnp.arange(NEAR))
    return far_part + near_part
```

```python
import functools

import jax
import jax.numpy as jnp
from jax import lax
from jax.experimental import pallas as pl
from jax.experimental.pallas import tpu as pltpu
from jax.sharding import PartitionSpec as P

highest = lax.Precision.HIGHEST
AXES = ("sx", "sy")
f32 = jnp.float32
bf16 = jnp.bfloat16
NN = (((1,), (0,)), ((), ()))
NT = (((1,), (1,)), ((), ()))


def mm(a, b, dims=NN, precision=None):
    return lax.dot_general(a, b, dims, precision=precision, preferred_element_type=f32)


def params(mib):
    return pltpu.CompilerParams(
        dimension_semantics=("arbitrary",), vmem_limit_bytes=mib * 1024 * 1024
    )


def moments_kernel(charges, basis, child, parent, send, box):
    step = pl.program_id(0)
    leaf_pairs = 8 * pl.num_programs(0)
    rank = basis.shape[1]
    parents = []
    for p in range(2):
        acc = None
        for i in range(4):
            c = 8 * p + 2 * i
            pair = jnp.concatenate(
                [mm(charges[c], basis[c], NT), mm(charges[c + 1], basis[c + 1], NT)], axis=1
            ).astype(bf16)
            send[step * 8 + p * 4 + i] = pair
            term = mm(pair, child[c : c + 2].reshape(2 * rank, rank))
            acc = term if acc is None else acc + term
        parents.append(acc)
    both = jnp.concatenate(parents, axis=1).astype(bf16)
    send[leaf_pairs + step] = both
    part = mm(both, parent[...].reshape(2 * rank, rank))

    @pl.when(step == 0)
    def _():
        box[...] = part

    @pl.when(step > 0)
    def _():
        box[...] += part


def moments_call(charges, basis, child, parent):
    leaves, columns, points = charges.shape
    rank = basis.shape[1]
    parents = parent.shape[0]
    steps = parents // 2
    pairs = leaves // 2 + parents // 2
    return pl.pallas_call(
        moments_kernel,
        grid=(steps,),
        in_specs=[
            pl.BlockSpec((16, columns, points), lambda i: (i, 0, 0)),
            pl.BlockSpec((16, rank, points), lambda i: (i, 0, 0)),
            pl.BlockSpec((16, rank, rank), lambda i: (i, 0, 0)),
            pl.BlockSpec((2, rank, rank), lambda i: (i, 0, 0)),
        ],
        out_specs=[
            pl.BlockSpec((pairs, columns, 2 * rank), lambda i: (0, 0, 0)),
            pl.BlockSpec((columns, rank), lambda i: (0, 0)),
        ],
        out_shape=[
            jax.ShapeDtypeStruct((pairs, columns, 2 * rank), bf16),
            jax.ShapeDtypeStruct((columns, rank), f32),
        ],
        compiler_params=params(32),
        name="moments",
    )(charges, basis, child, parent)


OPS_BLOCK = 128


def table_kernel(ops, table, turned):
    rank = ops.shape[1]
    half = rank // 2
    stride = turned.shape[0] // half
    for k in range(half):
        both = jnp.concatenate([ops[0, k], ops[0, k + half]], axis=0).astype(f32)
        turned[k * stride : k * stride + OPS_BLOCK, :] = both.T
    for o in range(OPS_BLOCK):
        rows = turned[pl.ds(o, half, stride=stride), :]
        table[0, o] = jnp.concatenate([rows[:, :rank], rows[:, rank:]], axis=0).astype(bf16)


def table_call(ops):
    levels, count, rank, _ = ops.shape
    blocks = pl.cdiv(count, OPS_BLOCK)
    turned_view = jnp.transpose(ops, (0, 2, 3, 1))
    return pl.pallas_call(
        table_kernel,
        grid=(levels, blocks),
        in_specs=[pl.BlockSpec((1, rank, rank, OPS_BLOCK), lambda t, i: (t, 0, 0, i))],
        out_specs=pl.BlockSpec((1, OPS_BLOCK, rank, rank), lambda t, i: (t, i, 0, 0)),
        out_shape=jax.ShapeDtypeStruct((levels, blocks * OPS_BLOCK, rank, rank), bf16),
        scratch_shapes=[pltpu.VMEM((rank // 2 * (OPS_BLOCK + 8), 2 * rank), f32)],
        compiler_params=pltpu.CompilerParams(
            dimension_semantics=("arbitrary", "arbitrary"), vmem_limit_bytes=32 * 1024 * 1024
        ),
        name="operator_table",
    )(turned_view)


NEAR_LEAVES = 8


def near_kernel(base, near, left, own, right, blocks, out, sources, sems):
    step = pl.program_id(0)
    leaves = own.shape[0]

    @pl.when(step == 0)
    def _():
        copies = [
            pltpu.make_async_copy(ref, sources.at[pl.ds(i * leaves, leaves)], sems.at[i])
            for i, ref in enumerate((left, own, right))
        ]
        for copy in copies:
            copy.start()
        for copy in copies:
            copy.wait()

    count = blocks.shape[1]
    for i in range(NEAR_LEAVES):
        row = step * NEAR_LEAVES + i
        acc = None
        for n in range(0, count, 2):
            lhs = jnp.concatenate(
                [sources[near[n, row] - base[0]], sources[near[n + 1, row] - base[0]]], axis=1
            )
            rhs = jnp.concatenate([blocks[i, n], blocks[i, n + 1]], axis=1)
            term = mm(lhs, rhs, NT)
            acc = term if acc is None else acc + term
        out[i] = acc


def near_call(base, near_rows, left, own, right, blocks):
    leaves, columns, points = own.shape
    count = blocks.shape[1]
    hbm = pl.BlockSpec(memory_space=pl.ANY)
    return pl.pallas_call(
        near_kernel,
        grid_spec=pltpu.PrefetchScalarGridSpec(
            num_scalar_prefetch=2,
            grid=(leaves // NEAR_LEAVES,),
            in_specs=[
                hbm,
                hbm,
                hbm,
                pl.BlockSpec((NEAR_LEAVES, count, points, points), lambda i, *_: (i, 0, 0, 0)),
            ],
            out_specs=pl.BlockSpec((NEAR_LEAVES, columns, points), lambda i, *_: (i, 0, 0)),
            scratch_shapes=[
                pltpu.VMEM((3 * leaves, columns, points), bf16),
                pltpu.SemaphoreType.DMA((3,)),
            ],
        ),
        out_shape=jax.ShapeDtypeStruct((leaves, columns, points), f32),
        compiler_params=params(32),
        name="near",
    )(base, near_rows, left, own, right, blocks)


def doubled(pair, low):
    rank = pair.shape[1] // 2
    swapped = jnp.concatenate([pair[:, rank:], pair[:, :rank]], axis=1)
    return jnp.where(low, pair, swapped), jnp.where(low, swapped, pair)


def translated(acc, sources, table, level, lists, ops, base, row, low):
    count = lists.shape[0]
    for e in range(0, count, 4):
        picked = [sources[lists[e + i, row] - base] for i in range(4)]
        lhs = jnp.concatenate(
            [jnp.where(low, picked[0], picked[1]), jnp.where(low, picked[2], picked[3])], axis=1
        )
        rhs = jnp.concatenate([table[level, ops[e + i, row]] for i in range(4)], axis=0)
        acc = acc + mm(lhs, rhs)
    return acc


def far_kernel(
    base, list0, op0, list1, op1,
    left, own, right, table, siblings, transfer, couple, parent, child, basis, near,
    out, leaf_sources, parent_sources, parent_locals,
):
    step = pl.program_id(0)
    parents = pl.num_programs(0)
    leaves = 8 * parents
    columns = own.shape[1]
    rank = own.shape[2] // 2
    low = lax.broadcasted_iota(jnp.int32, (columns, 2 * rank), 1) < rank

    @pl.when(step == 0)
    def _():
        for i, ref in enumerate((left, own, right)):
            def leaf_pair(n, _, i=i, ref=ref):
                a, b = doubled(ref[n], low)
                leaf_sources[i * leaves + 2 * n] = a
                leaf_sources[i * leaves + 2 * n + 1] = b
                return 0

            lax.fori_loop(0, leaves // 2, leaf_pair, 0)

            def parent_pair(n, _, i=i, ref=ref):
                a, b = doubled(ref[leaves // 2 + n], low)
                parent_sources[i * parents + 2 * n] = a
                parent_sources[i * parents + 2 * n + 1] = b
                return 0

            lax.fori_loop(0, parents // 2, parent_pair, 0)
        field = None
        for j in reversed(range(siblings.shape[0])):
            term = mm(siblings[j], couple[...], precision=highest)
            if field is not None:
                term = term + mm(field, transfer[...], NT, precision=highest)
            field = term
        box_local = field.astype(bf16)

        def one_parent(q, _):
            acc = mm(box_local, parent[q], NT)
            acc = translated(acc, parent_sources, table, 1, list1, op1, base[1], q, low)
            parent_locals[q] = acc.astype(bf16)
            return 0

        lax.fori_loop(0, parents, one_parent, 0)

    parent_local = parent_locals[step]
    for c in range(8):
        row = step * 8 + c
        acc = mm(parent_local, child[c], NT)
        acc = translated(acc, leaf_sources, table, 0, list0, op0, base[0], row, low)
        out[c] = near[c] + mm(acc.astype(bf16), basis[c])


def far_call(base, list0, op0, list1, op1, left, own, right, table, siblings, transfer, couple, parent, child, basis, near):
    leaves, rank, points = basis.shape
    parents = parent.shape[0]
    columns = near.shape[1]

    def whole(x):
        return pl.BlockSpec(x.shape, lambda i, *_: (0,) * x.ndim)

    def rows(x):
        return pl.BlockSpec((8,) + x.shape[1:], lambda i, *_: (i,) + (0,) * (x.ndim - 1))

    return pl.pallas_call(
        far_kernel,
        grid_spec=pltpu.PrefetchScalarGridSpec(
            num_scalar_prefetch=5,
            grid=(parents,),
            in_specs=[whole(x) for x in (left, own, right, table, siblings, transfer, couple, parent)]
            + [rows(x) for x in (child, basis, near)],
            out_specs=rows(near),
            scratch_shapes=[
                pltpu.VMEM((3 * leaves, columns, 2 * rank), bf16),
                pltpu.VMEM((3 * parents, columns, 2 * rank), bf16),
                pltpu.VMEM((parents, columns, rank), bf16),
            ],
        ),
        out_shape=jax.ShapeDtypeStruct((leaves, columns, points), f32),
        compiler_params=params(56),
        name="far",
    )(base, list0, op0, list1, op1, left, own, right, table, siblings, transfer, couple, parent, child, basis, near)


def to_right(block):
    count = lax.axis_size(AXES)
    return lax.ppermute(block, AXES, [(i, i + 1) for i in range(count - 1)])


def to_left(block):
    count = lax.axis_size(AXES)
    return lax.ppermute(block, AXES, [(i + 1, i) for i in range(count - 1)])


def from_partner(block, apart):
    count = lax.axis_size(AXES)
    return lax.ppermute(block, AXES, [(i, i ^ (1 << apart)) for i in range(count)])


def local(
    charges, near_blocks, near_list, leaf_basis, child_transfer, parent_transfer, m2l_ops,
    far_list0, far_op0, far_list1, far_op1, top_transfer, top_couple,
):
    leaves = charges.shape[0]
    parents = parent_transfer.shape[0]
    device = lax.axis_index(AXES)
    base = jnp.stack([(device - 1) * leaves, (device - 1) * parents]).astype(jnp.int32)
    charges_left = to_right(charges)
    charges_right = to_left(charges)
    send, box = moments_call(charges, leaf_basis, child_transfer, parent_transfer)
    moments_left = to_right(send)
    moments_right = to_left(send)
    height = lax.axis_size(AXES).bit_length() - 1
    siblings = []
    current = box
    for level_bit in range(height):
        partner = from_partner(current, level_bit)
        siblings.append(partner)
        if level_bit + 1 < height:
            current = mm(current + partner, top_transfer, precision=highest)
    table = table_call(m2l_ops)
    near = near_call(base, near_list.T, charges_left, charges, charges_right, near_blocks)
    return far_call(
        base, far_list0.T, far_op0.T, far_list1.T, far_op1.T,
        moments_left, send, moments_right, table, jnp.stack(siblings),
        top_transfer, top_couple, parent_transfer, child_transfer, leaf_basis, near,
    )


def solution(mesh):
    split = P(AXES)
    placed = (split,) * 6 + (P(),) + (split,) * 4 + (P(), P())
    return jax.shard_map(local, mesh=mesh, in_specs=placed, out_specs=split, check_vma=False)
```

```python
import functools

import jax
import jax.numpy as jnp
from jax import lax
from jax.experimental import pallas as pl
from jax.experimental.pallas import tpu as pltpu
from jax.sharding import PartitionSpec as P

highest = lax.Precision.HIGHEST
AXES = ("sx", "sy")
f32 = jnp.float32
bf16 = jnp.bfloat16
NN = (((1,), (0,)), ((), ()))
NT = (((1,), (1,)), ((), ()))


def mm(a, b, dims=NN, precision=None):
    return lax.dot_general(a, b, dims, precision=precision, preferred_element_type=f32)


def params(mib):
    return pltpu.CompilerParams(
        dimension_semantics=("arbitrary",), vmem_limit_bytes=mib * 1024 * 1024
    )


def moments_kernel(charges, basis, child, parent, send, box):
    step = pl.program_id(0)
    leaf_pairs = 8 * pl.num_programs(0)
    rank = basis.shape[1]
    pairs = [
        jnp.concatenate(
            [mm(charges[c], basis[c], NT), mm(charges[c + 1], basis[c + 1], NT)], axis=1
        ).astype(bf16)
        for c in range(0, 16, 2)
    ]
    parents = [
        mm(
            jnp.concatenate(pairs[4 * p : 4 * p + 4], axis=1),
            child[8 * p : 8 * p + 8].reshape(8 * rank, rank),
        )
        for p in range(2)
    ]
    for i, pair in enumerate(pairs):
        send[step * 8 + i] = pair
    both = jnp.concatenate(parents, axis=1).astype(bf16)
    send[leaf_pairs + step] = both
    part = mm(both, parent[...].reshape(2 * rank, rank))

    @pl.when(step == 0)
    def _():
        box[...] = part

    @pl.when(step > 0)
    def _():
        box[...] += part


def moments_call(charges, basis, child, parent):
    leaves, columns, points = charges.shape
    rank = basis.shape[1]
    parents = parent.shape[0]
    steps = parents // 2
    pairs = leaves // 2 + parents // 2
    return pl.pallas_call(
        moments_kernel,
        grid=(steps,),
        in_specs=[
            pl.BlockSpec((16, columns, points), lambda i: (i, 0, 0)),
            pl.BlockSpec((16, rank, points), lambda i: (i, 0, 0)),
            pl.BlockSpec((16, rank, rank), lambda i: (i, 0, 0)),
            pl.BlockSpec((2, rank, rank), lambda i: (i, 0, 0)),
        ],
        out_specs=[
            pl.BlockSpec((pairs, columns, 2 * rank), lambda i: (0, 0, 0)),
            pl.BlockSpec((columns, rank), lambda i: (0, 0)),
        ],
        out_shape=[
            jax.ShapeDtypeStruct((pairs, columns, 2 * rank), bf16),
            jax.ShapeDtypeStruct((columns, rank), f32),
        ],
        compiler_params=params(32),
        name="moments",
    )(charges, basis, child, parent)


OPS_BLOCK = 128


def table_kernel(ops, table, turned):
    rank = ops.shape[1]
    half = rank // 2
    stride = turned.shape[0] // half
    for k in range(half):
        both = jnp.concatenate([ops[0, k], ops[0, k + half]], axis=0).astype(f32)
        turned[k * stride : k * stride + OPS_BLOCK, :] = both.T
    for o in range(OPS_BLOCK):
        rows = turned[pl.ds(o, half, stride=stride), :]
        table[0, o] = jnp.concatenate([rows[:, :rank], rows[:, rank:]], axis=0).astype(bf16)


def table_call(ops):
    levels, count, rank, _ = ops.shape
    blocks = pl.cdiv(count, OPS_BLOCK)
    turned_view = jnp.transpose(ops, (0, 2, 3, 1))
    return pl.pallas_call(
        table_kernel,
        grid=(levels, blocks),
        in_specs=[pl.BlockSpec((1, rank, rank, OPS_BLOCK), lambda t, i: (t, 0, 0, i))],
        out_specs=pl.BlockSpec((1, OPS_BLOCK, rank, rank), lambda t, i: (t, i, 0, 0)),
        out_shape=jax.ShapeDtypeStruct((levels, blocks * OPS_BLOCK, rank, rank), bf16),
        scratch_shapes=[pltpu.VMEM((rank // 2 * (OPS_BLOCK + 8), 2 * rank), f32)],
        compiler_params=pltpu.CompilerParams(
            dimension_semantics=("arbitrary", "arbitrary"), vmem_limit_bytes=32 * 1024 * 1024
        ),
        name="operator_table",
    )(turned_view)


NEAR_LEAVES = 8


def near_kernel(base, near, left, own, right, blocks, far, out, sources, sems):
    step = pl.program_id(0)
    leaves = own.shape[0]

    @pl.when(step == 0)
    def _():
        copies = [
            pltpu.make_async_copy(ref, sources.at[pl.ds(i * leaves, leaves)], sems.at[i])
            for i, ref in enumerate((left, own, right))
        ]
        for copy in copies:
            copy.start()
        for copy in copies:
            copy.wait()

    count = blocks.shape[1]
    results = []
    for i in range(NEAR_LEAVES):
        row = step * NEAR_LEAVES + i
        acc = far[i]
        for n in range(0, count, 2):
            lhs = jnp.concatenate(
                [sources[near[n, row] - base[0]], sources[near[n + 1, row] - base[0]]], axis=1
            )
            rhs = jnp.concatenate([blocks[i, n], blocks[i, n + 1]], axis=1)
            acc = acc + mm(lhs, rhs, NT)
        results.append(acc)
    for i, acc in enumerate(results):
        out[i] = acc


def near_call(base, near_rows, left, own, right, blocks, far):
    leaves, columns, points = own.shape
    count = blocks.shape[1]
    hbm = pl.BlockSpec(memory_space=pl.ANY)
    return pl.pallas_call(
        near_kernel,
        grid_spec=pltpu.PrefetchScalarGridSpec(
            num_scalar_prefetch=2,
            grid=(leaves // NEAR_LEAVES,),
            in_specs=[
                hbm,
                hbm,
                hbm,
                pl.BlockSpec((NEAR_LEAVES, count, points, points), lambda i, *_: (i, 0, 0, 0)),
                pl.BlockSpec((NEAR_LEAVES, columns, points), lambda i, *_: (i, 0, 0)),
            ],
            out_specs=pl.BlockSpec((NEAR_LEAVES, columns, points), lambda i, *_: (i, 0, 0)),
            scratch_shapes=[
                pltpu.VMEM((3 * leaves, columns, points), bf16),
                pltpu.SemaphoreType.DMA((3,)),
            ],
        ),
        out_shape=jax.ShapeDtypeStruct((leaves, columns, points), f32),
        compiler_params=params(32),
        name="near",
    )(base, near_rows, left, own, right, blocks, far)


def doubled(pair, low):
    rank = pair.shape[1] // 2
    swapped = jnp.concatenate([pair[:, rank:], pair[:, :rank]], axis=1)
    return jnp.where(low, pair, swapped), jnp.where(low, swapped, pair)


def translated(acc, sources, table, lists, ops, base, row, low):
    count = lists.shape[0]
    for e in range(0, count, 4):
        picked = [sources[lists[e + i, row] - base] for i in range(4)]
        lhs = jnp.concatenate(
            [jnp.where(low, picked[0], picked[1]), jnp.where(low, picked[2], picked[3])], axis=1
        )
        rhs = jnp.concatenate([table[ops[e + i, row]] for i in range(4)], axis=0)
        acc = acc + mm(lhs, rhs)
    return acc


def far_kernel(
    base, list0, op0, list1, op1,
    left, own, right, table, siblings, transfer, couple, parent, child, basis,
    out, leaf_sources, parent_sources, parent_locals, leaf_table, parent_table, sems,
):
    step = pl.program_id(0)
    parents = pl.num_programs(0)
    leaves = leaf_sources.shape[0] // 3
    columns = own.shape[1]
    rank = own.shape[2] // 2
    low = lax.broadcasted_iota(jnp.int32, (columns, 2 * rank), 1) < rank

    @pl.when(step == 0)
    def _():
        ops = leaf_table.shape[0]
        parent_copy = pltpu.make_async_copy(table.at[1, pl.ds(0, ops)], parent_table, sems.at[0])
        leaf_copy = pltpu.make_async_copy(table.at[0, pl.ds(0, ops)], leaf_table, sems.at[1])
        parent_copy.start()
        leaf_copy.start()
        for i, ref in enumerate((left, own, right)):
            for n in range(leaves // 2):
                a, b = doubled(ref[n], low)
                leaf_sources[i * leaves + 2 * n] = a
                leaf_sources[i * leaves + 2 * n + 1] = b
            for n in range(leaves // 16):
                a, b = doubled(ref[leaves // 2 + n], low)
                parent_sources[i * leaves // 8 + 2 * n] = a
                parent_sources[i * leaves // 8 + 2 * n + 1] = b
        field = None
        for j in reversed(range(siblings.shape[0])):
            term = mm(siblings[j], couple[...], precision=highest)
            if field is not None:
                term = term + mm(field, transfer[...], NT, precision=highest)
            field = term
        box_local = field.astype(bf16)
        parent_copy.wait()
        accs = [
            translated(mm(box_local, parent[q], NT), parent_sources, parent_table, list1, op1, base[1], q, low)
            for q in range(leaves // 8)
        ]
        for q, acc in enumerate(accs):
            parent_locals[q] = acc.astype(bf16)
        leaf_copy.wait()

    parent_local = parent_locals[step]
    accs = [
        translated(mm(parent_local, child[c], NT), leaf_sources, leaf_table, list0, op0, base[0], step * 8 + c, low)
        for c in range(8)
    ]
    results = [mm(acc.astype(bf16), basis[c]) for c, acc in enumerate(accs)]
    for c, acc in enumerate(results):
        out[c] = acc


def far_call(base, list0, op0, list1, op1, left, own, right, table, count, siblings, transfer, couple, parent, child, basis):
    leaves, rank, points = basis.shape
    parents = parent.shape[0]
    columns = own.shape[1]

    def whole(x):
        return pl.BlockSpec(x.shape, lambda i, *_: (0,) * x.ndim)

    def rows(shape):
        return pl.BlockSpec((8,) + shape[1:], lambda i, *_: (i,) + (0,) * (len(shape) - 1))

    return pl.pallas_call(
        far_kernel,
        grid_spec=pltpu.PrefetchScalarGridSpec(
            num_scalar_prefetch=5,
            grid=(parents,),
            in_specs=[whole(x) for x in (left, own, right)]
            + [pl.BlockSpec(memory_space=pl.ANY)]
            + [whole(x) for x in (siblings, transfer, couple, parent)]
            + [rows(x.shape) for x in (child, basis)],
            out_specs=rows((leaves, columns, points)),
            scratch_shapes=[
                pltpu.VMEM((3 * leaves, columns, 2 * rank), bf16),
                pltpu.VMEM((3 * parents, columns, 2 * rank), bf16),
                pltpu.VMEM((parents, columns, rank), bf16),
                pltpu.VMEM((count, rank, rank), bf16),
                pltpu.VMEM((count, rank, rank), bf16),
                pltpu.SemaphoreType.DMA((2,)),
            ],
        ),
        out_shape=jax.ShapeDtypeStruct((leaves, columns, points), f32),
        compiler_params=params(40),
        name="far",
    )(base, list0, op0, list1, op1, left, own, right, table, siblings, transfer, couple, parent, child, basis)


def to_right(block):
    count = lax.axis_size(AXES)
    return lax.ppermute(block, AXES, [(i, i + 1) for i in range(count - 1)])


def to_left(block):
    count = lax.axis_size(AXES)
    return lax.ppermute(block, AXES, [(i + 1, i) for i in range(count - 1)])


def from_partner(block, apart):
    count = lax.axis_size(AXES)
    return lax.ppermute(block, AXES, [(i, i ^ (1 << apart)) for i in range(count)])


def local(
    charges, near_blocks, near_list, leaf_basis, child_transfer, parent_transfer, m2l_ops,
    far_list0, far_op0, far_list1, far_op1, top_transfer, top_couple,
):
    leaves = charges.shape[0]
    parents = parent_transfer.shape[0]
    device = lax.axis_index(AXES)
    base = jnp.stack([(device - 1) * leaves, (device - 1) * parents]).astype(jnp.int32)
    charges_left = to_right(charges)
    charges_right = to_left(charges)
    send, box = moments_call(charges, leaf_basis, child_transfer, parent_transfer)
    moments_left = to_right(send)
    moments_right = to_left(send)
    height = lax.axis_size(AXES).bit_length() - 1
    siblings = []
    current = box
    for level_bit in range(height):
        partner = from_partner(current, level_bit)
        siblings.append(partner)
        if level_bit + 1 < height:
            current = mm(current + partner, top_transfer, precision=highest)
    table = table_call(m2l_ops)
    far = far_call(
        base, far_list0.T, far_op0.T, far_list1.T, far_op1.T,
        moments_left, send, moments_right, table, m2l_ops.shape[1], jnp.stack(siblings),
        top_transfer, top_couple, parent_transfer, child_transfer, leaf_basis,
    )
    return near_call(base, near_list.T, charges_left, charges, charges_right, near_blocks, far)


def solution(mesh):
    split = P(AXES)
    placed = (split,) * 6 + (P(),) + (split,) * 4 + (P(), P())
    return jax.shard_map(local, mesh=mesh, in_specs=placed, out_specs=split, check_vma=False)
```

```python
import functools

import jax
import jax.numpy as jnp
from jax import lax
from jax.experimental import pallas as pl
from jax.experimental.pallas import tpu as pltpu
from jax.sharding import PartitionSpec as P

highest = lax.Precision.HIGHEST
AXES = ("sx", "sy")
f32 = jnp.float32
bf16 = jnp.bfloat16
NN = (((1,), (0,)), ((), ()))
NT = (((1,), (1,)), ((), ()))


def mm(a, b, dims=NN, precision=None):
    return lax.dot_general(a, b, dims, precision=precision, preferred_element_type=f32)


def in_hbm(x):
    return pltpu.with_memory_space_constraint(x, pltpu.HBM)


VMEM = pl.BlockSpec(memory_space=pltpu.VMEM)


def params(mib):
    return pltpu.CompilerParams(
        dimension_semantics=("arbitrary",), vmem_limit_bytes=mib * 1024 * 1024
    )


def moments_kernel(charges, basis, child, parent, send, box):
    step = pl.program_id(0)
    leaf_pairs = 8 * pl.num_programs(0)
    rank = basis.shape[1]
    pairs = [
        jnp.concatenate(
            [mm(charges[c], basis[c], NT), mm(charges[c + 1], basis[c + 1], NT)], axis=1
        ).astype(bf16)
        for c in range(0, 16, 2)
    ]
    parents = [
        mm(
            jnp.concatenate(pairs[4 * p : 4 * p + 4], axis=1),
            child[8 * p : 8 * p + 8].reshape(8 * rank, rank),
        )
        for p in range(2)
    ]
    for i, pair in enumerate(pairs):
        send[step * 8 + i] = pair
    both = jnp.concatenate(parents, axis=1).astype(bf16)
    send[leaf_pairs + step] = both
    part = mm(both, parent[...].reshape(2 * rank, rank))

    @pl.when(step == 0)
    def _():
        box[...] = part

    @pl.when(step > 0)
    def _():
        box[...] += part


def moments_call(charges, basis, child, parent):
    leaves, columns, points = charges.shape
    rank = basis.shape[1]
    parents = parent.shape[0]
    steps = parents // 2
    pairs = leaves // 2 + parents // 2
    return pl.pallas_call(
        moments_kernel,
        grid=(steps,),
        in_specs=[
            pl.BlockSpec((16, columns, points), lambda i: (i, 0, 0)),
            pl.BlockSpec((16, rank, points), lambda i: (i, 0, 0)),
            pl.BlockSpec((16, rank, rank), lambda i: (i, 0, 0)),
            pl.BlockSpec((2, rank, rank), lambda i: (i, 0, 0)),
        ],
        out_specs=[
            pl.BlockSpec((pairs, columns, 2 * rank), lambda i: (0, 0, 0)),
            pl.BlockSpec((columns, rank), lambda i: (0, 0)),
        ],
        out_shape=[
            jax.ShapeDtypeStruct((pairs, columns, 2 * rank), bf16),
            jax.ShapeDtypeStruct((columns, rank), f32),
        ],
        compiler_params=params(16),
        name="moments",
    )(in_hbm(charges), in_hbm(basis), in_hbm(child), in_hbm(parent))


OPS_BLOCK = 128


def table_kernel(ops, table, turned):
    level = pl.program_id(0)
    first = pl.program_id(1) * OPS_BLOCK
    rank = ops.shape[1]
    half = rank // 2
    stride = turned.shape[0] // half
    for k in range(half):
        both = jnp.concatenate([ops[0, k], ops[0, k + half]], axis=0).astype(f32)
        turned[k * stride : k * stride + OPS_BLOCK, :] = both.T
    for o in range(OPS_BLOCK):
        rows = turned[pl.ds(o, half, stride=stride), :]
        table[level, first + o] = jnp.concatenate([rows[:, :rank], rows[:, rank:]], axis=0).astype(bf16)


def table_call(ops):
    levels, count, rank, _ = ops.shape
    blocks = pl.cdiv(count, OPS_BLOCK)
    turned_view = jnp.transpose(ops, (0, 2, 3, 1))
    return pl.pallas_call(
        table_kernel,
        grid=(levels, blocks),
        in_specs=[pl.BlockSpec((1, rank, rank, OPS_BLOCK), lambda t, i: (t, 0, 0, i))],
        out_specs=VMEM,
        out_shape=jax.ShapeDtypeStruct((levels, blocks * OPS_BLOCK, rank, rank), bf16),
        scratch_shapes=[pltpu.VMEM((rank // 2 * (OPS_BLOCK + 8), 2 * rank), f32)],
        compiler_params=pltpu.CompilerParams(
            dimension_semantics=("arbitrary", "arbitrary"), vmem_limit_bytes=16 * 1024 * 1024
        ),
        name="operator_table",
    )(in_hbm(turned_view))


NEAR_LEAVES = 8


def near_kernel(base, near, left, own, right, blocks, far, out, sources):
    step = pl.program_id(0)
    leaves = own.shape[0]

    @pl.when(step == 0)
    def _():
        for i, ref in enumerate((left, own, right)):
            for n in range(0, leaves, 8):
                sources[i * leaves + n : i * leaves + n + 8] = ref[n : n + 8]

    count = blocks.shape[1]
    results = []
    for i in range(NEAR_LEAVES):
        row = step * NEAR_LEAVES + i
        acc = far[i]
        for n in range(0, count, 2):
            lhs = jnp.concatenate(
                [sources[near[n, row] - base[0]], sources[near[n + 1, row] - base[0]]], axis=1
            )
            rhs = jnp.concatenate([blocks[i, n], blocks[i, n + 1]], axis=1)
            acc = acc + mm(lhs, rhs, NT)
        results.append(acc)
    for i, acc in enumerate(results):
        out[i] = acc


def near_call(base, near_rows, left, own, right, blocks, far):
    leaves, columns, points = own.shape
    count = blocks.shape[1]
    return pl.pallas_call(
        near_kernel,
        grid_spec=pltpu.PrefetchScalarGridSpec(
            num_scalar_prefetch=2,
            grid=(leaves // NEAR_LEAVES,),
            in_specs=[
                VMEM,
                VMEM,
                VMEM,
                pl.BlockSpec((NEAR_LEAVES, count, points, points), lambda i, *_: (i, 0, 0, 0)),
                pl.BlockSpec((NEAR_LEAVES, columns, points), lambda i, *_: (i, 0, 0)),
            ],
            out_specs=pl.BlockSpec((NEAR_LEAVES, columns, points), lambda i, *_: (i, 0, 0)),
            scratch_shapes=[
                pltpu.VMEM((3 * leaves, columns, points), bf16),
            ],
        ),
        out_shape=jax.ShapeDtypeStruct((leaves, columns, points), f32),
        compiler_params=params(16),
        name="near",
    )(base, near_rows, left, own, right, in_hbm(blocks), far)


def doubled(pair, low):
    rank = pair.shape[1] // 2
    swapped = jnp.concatenate([pair[:, rank:], pair[:, :rank]], axis=1)
    return jnp.where(low, pair, swapped), jnp.where(low, swapped, pair)


def translated(acc, sources, table, level, lists, ops, base, at, low):
    for e in range(0, len(at), 4):
        picked = [sources[lists[at[e + i]] - base] for i in range(4)]
        lhs = jnp.concatenate(
            [jnp.where(low, picked[0], picked[1]), jnp.where(low, picked[2], picked[3])], axis=1
        )
        rhs = jnp.concatenate([table[level, ops[at[e + i]]] for i in range(4)], axis=0)
        acc = acc + mm(lhs, rhs)
    return acc


def far_kernel(
    base, list0, op0, list1, op1,
    left, own, right, table, transfer, couple, parent, child, basis, *rest,
):
    siblings = rest[:-4]
    out, leaf_sources, parent_sources, parent_locals = rest[-4:]
    leaves = basis.shape[0]
    parents = parent.shape[0]
    columns = own.shape[1]
    rank = own.shape[2] // 2
    low = lax.broadcasted_iota(jnp.int32, (columns, 2 * rank), 1) < rank
    for i, ref in enumerate((left, own, right)):
        for n in range(leaves // 2):
            a, b = doubled(ref[n], low)
            leaf_sources[i * leaves + 2 * n] = a
            leaf_sources[i * leaves + 2 * n + 1] = b
        for n in range(parents // 2):
            a, b = doubled(ref[leaves // 2 + n], low)
            parent_sources[i * parents + 2 * n] = a
            parent_sources[i * parents + 2 * n + 1] = b
    field = None
    for sibling in reversed(siblings):
        term = mm(sibling[...], couple[...], precision=highest)
        if field is not None:
            term = term + mm(field, transfer[...], NT, precision=highest)
        field = term
    box_local = field.astype(bf16)
    accs = [
        translated(
            mm(box_local, parent[q], NT), parent_sources, table, 1, list1, op1, base[1],
            [(q, e) for e in range(list1.shape[1])], low,
        )
        for q in range(parents)
    ]
    for q, acc in enumerate(accs):
        parent_locals[q] = acc.astype(bf16)

    def one_parent(q, _):
        parent_local = parent_locals[q]
        accs = [
            translated(
                mm(parent_local, child[q * 8 + c], NT), leaf_sources, table, 0, list0, op0, base[0],
                [(e, q * 8 + c) for e in range(list0.shape[0])], low,
            )
            for c in range(8)
        ]
        results = [mm(acc.astype(bf16), basis[q * 8 + c]) for c, acc in enumerate(accs)]
        for c, acc in enumerate(results):
            out[q * 8 + c] = acc
        return 0

    lax.fori_loop(0, parents, one_parent, 0)


def far_call(base, list0, op0, list1, op1, left, own, right, table, siblings, transfer, couple, parent, child, basis):
    leaves, rank, points = basis.shape
    parents = parent.shape[0]
    columns = own.shape[1]
    smem = pl.BlockSpec(memory_space=pltpu.SMEM)
    return pl.pallas_call(
        far_kernel,
        in_specs=[smem] * 5 + [VMEM] * (9 + len(siblings)),
        out_specs=VMEM,
        scratch_shapes=[
            pltpu.VMEM((3 * leaves, columns, 2 * rank), bf16),
            pltpu.VMEM((3 * parents, columns, 2 * rank), bf16),
            pltpu.VMEM((parents, columns, rank), bf16),
        ],
        out_shape=jax.ShapeDtypeStruct((leaves, columns, points), f32),
        compiler_params=pltpu.CompilerParams(vmem_limit_bytes=16 * 1024 * 1024),
        name="far",
    )(base, list0, op0, list1, op1, left, own, right, table, transfer, couple, parent, child, basis, *siblings)


def to_right(block):
    count = lax.axis_size(AXES)
    return lax.ppermute(block, AXES, [(i, i + 1) for i in range(count - 1)])


def to_left(block):
    count = lax.axis_size(AXES)
    return lax.ppermute(block, AXES, [(i + 1, i) for i in range(count - 1)])


def from_partner(block, apart):
    count = lax.axis_size(AXES)
    return lax.ppermute(block, AXES, [(i, i ^ (1 << apart)) for i in range(count)])


def local(
    charges, near_blocks, near_list, leaf_basis, child_transfer, parent_transfer, m2l_ops,
    far_list0, far_op0, far_list1, far_op1, top_transfer, top_couple,
):
    leaves = charges.shape[0]
    parents = parent_transfer.shape[0]
    device = lax.axis_index(AXES)
    base = jnp.stack([(device - 1) * leaves, (device - 1) * parents]).astype(jnp.int32)
    send, box = moments_call(charges, leaf_basis, child_transfer, parent_transfer)
    height = lax.axis_size(AXES).bit_length() - 1
    siblings = []
    current = box
    for level_bit in range(height):
        if level_bit == 2:
            send, current = lax.optimization_barrier((send, current))
            moments_left = to_right(send)
            moments_right = to_left(send)
        partner = from_partner(current, level_bit)
        if level_bit == 2:
            charges_left = to_right(charges)
            charges_right = to_left(charges)
        siblings.append(partner)
        if level_bit + 1 < height:
            current = mm(current + partner, top_transfer, precision=highest)
    table = table_call(m2l_ops)
    far = far_call(
        base, far_list0.T, far_op0.T, far_list1, far_op1,
        moments_left, send, moments_right, table, siblings,
        top_transfer, top_couple, parent_transfer, child_transfer, leaf_basis,
    )
    return near_call(base, near_list.T, charges_left, charges, charges_right, near_blocks, far)


def solution(mesh):
    split = P(AXES)
    placed = (split,) * 6 + (P(),) + (split,) * 4 + (P(), P())
    return jax.shard_map(local, mesh=mesh, in_specs=placed, out_specs=split, check_vma=False)
```

```python
import functools

import jax
import jax.numpy as jnp
from jax import lax
from jax.experimental import pallas as pl
from jax.experimental.pallas import tpu as pltpu
from jax.sharding import PartitionSpec as P

highest = lax.Precision.HIGHEST
AXES = ("sx", "sy")
f32 = jnp.float32
bf16 = jnp.bfloat16
NN = (((1,), (0,)), ((), ()))
NT = (((1,), (1,)), ((), ()))


def mm(a, b, dims=NN, precision=None):
    return lax.dot_general(a, b, dims, precision=precision, preferred_element_type=f32)


def in_hbm(x):
    return pltpu.with_memory_space_constraint(x, pltpu.HBM)


VMEM = pl.BlockSpec(memory_space=pltpu.VMEM)
HBM = pl.BlockSpec(memory_space=pltpu.HBM)
SMEM = pl.BlockSpec(memory_space=pltpu.SMEM)


def params(mib):
    return pltpu.CompilerParams(
        dimension_semantics=("arbitrary",), vmem_limit_bytes=mib * 1024 * 1024
    )


def moments_kernel(charges, basis, child, parent, send, box):
    step = pl.program_id(0)
    leaf_pairs = 8 * pl.num_programs(0)
    rank = basis.shape[1]
    pairs = [
        jnp.concatenate(
            [mm(charges[c], basis[c], NT), mm(charges[c + 1], basis[c + 1], NT)], axis=1
        ).astype(bf16)
        for c in range(0, 16, 2)
    ]
    parents = [
        mm(
            jnp.concatenate(pairs[4 * p : 4 * p + 4], axis=1),
            child[8 * p : 8 * p + 8].reshape(8 * rank, rank),
        )
        for p in range(2)
    ]
    for i, pair in enumerate(pairs):
        send[step * 8 + i] = pair
    both = jnp.concatenate(parents, axis=1).astype(bf16)
    send[leaf_pairs + step] = both
    part = mm(both, parent[...].reshape(2 * rank, rank))

    @pl.when(step == 0)
    def _():
        box[...] = part

    @pl.when(step > 0)
    def _():
        box[...] += part


def moments_call(charges, basis, child, parent):
    leaves, columns, points = charges.shape
    rank = basis.shape[1]
    parents = parent.shape[0]
    steps = parents // 2
    pairs = leaves // 2 + parents // 2
    return pl.pallas_call(
        moments_kernel,
        grid=(steps,),
        in_specs=[
            pl.BlockSpec((16, columns, points), lambda i: (i, 0, 0)),
            pl.BlockSpec((16, rank, points), lambda i: (i, 0, 0)),
            pl.BlockSpec((16, rank, rank), lambda i: (i, 0, 0)),
            pl.BlockSpec((2, rank, rank), lambda i: (i, 0, 0)),
        ],
        out_specs=[
            pl.BlockSpec((pairs, columns, 2 * rank), lambda i: (0, 0, 0)),
            pl.BlockSpec((columns, rank), lambda i: (0, 0)),
        ],
        out_shape=[
            pltpu.HBM((pairs, columns, 2 * rank), bf16),
            jax.ShapeDtypeStruct((columns, rank), f32),
        ],
        compiler_params=params(16),
        name="moments",
    )(in_hbm(charges), in_hbm(basis), in_hbm(child), in_hbm(parent))


OPS_BLOCK = 128


def table_kernel(count, ops, transfer, couple, table, chain, turned):
    rank = ops.shape[1]
    half = rank // 2
    stride = turned.shape[0] // half
    level = pl.program_id(0)
    first = pl.program_id(1) * OPS_BLOCK

    @pl.when((level == 0) & (first == 0))
    def _():
        link = couple[...]
        chain[0] = link
        for j in range(1, chain.shape[0]):
            link = mm(mm(transfer[...], link, precision=highest), transfer[...], NT, precision=highest)
            chain[j] = link

    for k in range(half):
        both = jnp.concatenate([ops[0, k], ops[0, k + half]], axis=0).astype(f32)
        turned[k * stride : k * stride + OPS_BLOCK, :] = both.T

    def rows_of(start, stop):
        for o in range(start, stop):
            rows = turned[pl.ds(o, half, stride=stride), :]
            table[0, o] = jnp.concatenate([rows[:, :rank], rows[:, rank:]], axis=0).astype(bf16)

    rows_of(0, count % OPS_BLOCK)

    @pl.when(first + OPS_BLOCK <= count)
    def _():
        rows_of(count % OPS_BLOCK, OPS_BLOCK)


def table_call(ops, transfer, couple, links):
    levels, count, rank, _ = ops.shape
    return pl.pallas_call(
        functools.partial(table_kernel, count),
        grid=(levels, pl.cdiv(count, OPS_BLOCK)),
        in_specs=[pl.BlockSpec((1, rank, rank, OPS_BLOCK), lambda t, i: (t, 0, 0, i)), VMEM, VMEM],
        out_specs=[pl.BlockSpec((1, OPS_BLOCK, rank, rank), lambda t, i: (t, i, 0, 0)), VMEM],
        out_shape=[
            pltpu.HBM((levels, count, rank, rank), bf16),
            jax.ShapeDtypeStruct((links, rank, rank), f32),
        ],
        scratch_shapes=[pltpu.VMEM((rank // 2 * (OPS_BLOCK + 8), 2 * rank), f32)],
        compiler_params=pltpu.CompilerParams(
            dimension_semantics=("arbitrary", "arbitrary"), vmem_limit_bytes=16 * 1024 * 1024
        ),
        name="operator_table",
    )(in_hbm(jnp.transpose(ops, (0, 2, 3, 1))), transfer, couple)


NEAR_LEAVES = 8


def near_kernel(base, near, left, own, right, blocks, far, out, sources, block_buf, out_buf, halo_sems, in_sems, out_sems):
    leaves = own.shape[0]
    count = blocks.shape[1]
    chunks = leaves // NEAR_LEAVES

    def fetch(c):
        rows = pl.ds(c * NEAR_LEAVES, NEAR_LEAVES)
        return pltpu.make_async_copy(blocks.at[rows], block_buf.at[rows], in_sems.at[c])

    def store(c):
        rows = pl.ds(c * NEAR_LEAVES, NEAR_LEAVES)
        return pltpu.make_async_copy(out_buf.at[rows], out.at[rows], out_sems.at[c])

    halo = [
        pltpu.make_async_copy(ref, sources.at[pl.ds(i * leaves, leaves)], halo_sems.at[i])
        for i, ref in enumerate((left, own, right))
    ]
    for copy in halo:
        copy.start()
    for c in range(chunks):
        fetch(c).start()
    for copy in halo:
        copy.wait()

    def one_chunk(c, _):
        fetch(c).wait()
        results = []
        for i in range(NEAR_LEAVES):
            row = c * NEAR_LEAVES + i
            acc = far[row]
            for n in range(0, count, 2):
                lhs = jnp.concatenate(
                    [sources[near[n, row] - base[0]], sources[near[n + 1, row] - base[0]]], axis=1
                )
                rhs = jnp.concatenate([block_buf[row, n], block_buf[row, n + 1]], axis=1)
                acc = acc + mm(lhs, rhs, NT)
            results.append(acc)
        for i, acc in enumerate(results):
            out_buf[c * NEAR_LEAVES + i] = acc
        store(c).start()
        return 0

    lax.fori_loop(0, chunks, one_chunk, 0)
    for c in range(chunks):
        store(c).wait()


def near_call(base, near_rows, left, own, right, blocks, far):
    leaves, columns, points = own.shape
    chunks = leaves // NEAR_LEAVES
    return pl.pallas_call(
        near_kernel,
        in_specs=[SMEM, SMEM, HBM, HBM, HBM, HBM, VMEM],
        out_specs=HBM,
        scratch_shapes=[
            pltpu.VMEM((3 * leaves, columns, points), bf16),
            pltpu.VMEM(blocks.shape, bf16),
            pltpu.VMEM((leaves, columns, points), f32),
            pltpu.SemaphoreType.DMA((3,)),
            pltpu.SemaphoreType.DMA((chunks,)),
            pltpu.SemaphoreType.DMA((chunks,)),
        ],
        out_shape=jax.ShapeDtypeStruct((leaves, columns, points), f32),
        compiler_params=pltpu.CompilerParams(vmem_limit_bytes=24 * 1024 * 1024),
        name="near",
    )(base, near_rows, in_hbm(left), in_hbm(own), in_hbm(right), in_hbm(blocks), far)


def doubled(pair, low):
    rank = pair.shape[1] // 2
    swapped = jnp.concatenate([pair[:, rank:], pair[:, :rank]], axis=1)
    return jnp.where(low, pair, swapped), jnp.where(low, swapped, pair)


def translated(acc, sources, table, lists, ops, base, at, low):
    for e in range(0, len(at), 4):
        picked = [sources[lists[at[e + i]] - base] for i in range(4)]
        lhs = jnp.concatenate(
            [jnp.where(low, picked[0], picked[1]), jnp.where(low, picked[2], picked[3])], axis=1
        )
        rhs = jnp.concatenate([table[ops[at[e + i]]] for i in range(4)], axis=0)
        acc = acc + mm(lhs, rhs)
    return acc


def far_kernel(
    base, list0, op0, list1, op1,
    left, own, right, table, chain, parent, child, basis, *rest,
):
    siblings = rest[:-8]
    out, halo, leaf_sources, parent_sources, parent_locals, leaf_table, parent_table, sems = rest[-8:]
    leaves = basis.shape[0]
    parents = parent.shape[0]
    columns = own.shape[1]
    rank = own.shape[2] // 2
    low = lax.broadcasted_iota(jnp.int32, (columns, 2 * rank), 1) < rank
    copies = [
        pltpu.make_async_copy(source, target, sems.at[i])
        for i, (source, target) in enumerate(
            [
                (own, halo.at[1]),
                (left, halo.at[0]),
                (right, halo.at[2]),
                (table.at[1], parent_table),
                (table.at[0], leaf_table),
            ]
        )
    ]
    for copy in copies:
        copy.start()
    field = mm(siblings[0][...], chain[0], precision=highest)
    for j in range(1, len(siblings)):
        field = field + mm(siblings[j][...], chain[j], precision=highest)
    box_local = field.astype(bf16)
    for copy, i in zip(copies, (1, 0, 2)):
        copy.wait()
        for n in range(leaves // 2):
            a, b = doubled(halo[i, n], low)
            leaf_sources[i * leaves + 2 * n] = a
            leaf_sources[i * leaves + 2 * n + 1] = b
        for n in range(parents // 2):
            a, b = doubled(halo[i, leaves // 2 + n], low)
            parent_sources[i * parents + 2 * n] = a
            parent_sources[i * parents + 2 * n + 1] = b
    copies[3].wait()
    accs = [
        translated(
            mm(box_local, parent[q], NT), parent_sources, parent_table, list1, op1, base[1],
            [(q, e) for e in range(list1.shape[1])], low,
        )
        for q in range(parents)
    ]
    for q, acc in enumerate(accs):
        parent_locals[q] = acc.astype(bf16)
    copies[4].wait()

    def one_parent(q, _):
        parent_local = parent_locals[q]
        accs = [
            translated(
                mm(parent_local, child[q * 8 + c], NT), leaf_sources, leaf_table, list0, op0, base[0],
                [(e, q * 8 + c) for e in range(list0.shape[0])], low,
            )
            for c in range(8)
        ]
        results = [mm(acc.astype(bf16), basis[q * 8 + c]) for c, acc in enumerate(accs)]
        for c, acc in enumerate(results):
            out[q * 8 + c] = acc
        return 0

    lax.fori_loop(0, parents, one_parent, 0)


def far_call(base, list0, op0, list1, op1, left, own, right, table, siblings, chain, parent, child, basis):
    leaves, rank, points = basis.shape
    parents = parent.shape[0]
    columns = own.shape[1]
    return pl.pallas_call(
        far_kernel,
        in_specs=[SMEM] * 5 + [HBM] * 4 + [VMEM] * (4 + len(siblings)),
        out_specs=VMEM,
        scratch_shapes=[
            pltpu.VMEM((3,) + own.shape, bf16),
            pltpu.VMEM((3 * leaves, columns, 2 * rank), bf16),
            pltpu.VMEM((3 * parents, columns, 2 * rank), bf16),
            pltpu.VMEM((parents, columns, rank), bf16),
            pltpu.VMEM(table.shape[1:], bf16),
            pltpu.VMEM(table.shape[1:], bf16),
            pltpu.SemaphoreType.DMA((5,)),
        ],
        out_shape=jax.ShapeDtypeStruct((leaves, columns, points), f32),
        compiler_params=pltpu.CompilerParams(vmem_limit_bytes=32 * 1024 * 1024),
        name="far",
    )(base, list0, op0, list1, op1, in_hbm(left), in_hbm(own), in_hbm(right), in_hbm(table), chain, parent, child, basis, *siblings)


def to_right(block):
    count = lax.axis_size(AXES)
    return lax.ppermute(block, AXES, [(i, i + 1) for i in range(count - 1)])


def to_left(block):
    count = lax.axis_size(AXES)
    return lax.ppermute(block, AXES, [(i + 1, i) for i in range(count - 1)])


def from_partner(block, apart):
    count = lax.axis_size(AXES)
    return lax.ppermute(block, AXES, [(i, i ^ (1 << apart)) for i in range(count)])


def after(x, *arrived):
    for y in arrived:
        x = x + jnp.minimum(jnp.abs(y[0, 0, 0].astype(f32)), 0.0)
    return x


def local(
    charges, near_blocks, near_list, leaf_basis, child_transfer, parent_transfer, m2l_ops,
    far_list0, far_op0, far_list1, far_op1, top_transfer, top_couple,
):
    leaves = charges.shape[0]
    parents = parent_transfer.shape[0]
    device = lax.axis_index(AXES)
    base = jnp.stack([(device - 1) * leaves, (device - 1) * parents]).astype(jnp.int32)
    height = lax.axis_size(AXES).bit_length() - 1
    tie = lax.optimization_barrier
    charges_left = to_right(charges)
    send, total = moments_call(charges, leaf_basis, child_transfer, parent_transfer)
    siblings = []
    for level in range(height):
        if level == 1:
            total, ops = tie((total, m2l_ops))
            table, chain = table_call(ops, top_transfer, top_couple, height)
        if level == 2:
            total, send = tie((after(total, charges_left), send))
            moments_left = to_right(send)
            moments_right = to_left(send)
        if level == height - 1:
            total, charges = tie((after(total, moments_left, moments_right), charges))
            charges_right = to_left(charges)
        partner = from_partner(total, level)
        if level == 1:
            partner, chain = tie((partner, chain))
        siblings.append(partner)
        total = total + partner
    far = far_call(
        base, far_list0.T, far_op0.T, far_list1, far_op1,
        moments_left, send, moments_right, table, siblings,
        chain, parent_transfer, child_transfer, leaf_basis,
    )
    return near_call(base, near_list.T, charges_left, charges, charges_right, near_blocks, far)


def solution(mesh):
    split = P(AXES)
    placed = (split,) * 6 + (P(),) + (split,) * 4 + (P(), P())
    return jax.shard_map(local, mesh=mesh, in_specs=placed, out_specs=split, check_vma=False)
```

```python
import functools

import jax
import jax.numpy as jnp
from jax import lax
from jax.experimental import pallas as pl
from jax.experimental.pallas import tpu as pltpu
from jax.sharding import PartitionSpec as P

highest = lax.Precision.HIGHEST
AXES = ("sx", "sy")
f32 = jnp.float32
bf16 = jnp.bfloat16
NN = (((1,), (0,)), ((), ()))
NT = (((1,), (1,)), ((), ()))


def mm(a, b, dims=NN, precision=None):
    return lax.dot_general(a, b, dims, precision=precision, preferred_element_type=f32)


def in_hbm(x):
    return pltpu.with_memory_space_constraint(x, pltpu.HBM)


VMEM = pl.BlockSpec(memory_space=pltpu.VMEM)
HBM = pl.BlockSpec(memory_space=pltpu.HBM)
SMEM = pl.BlockSpec(memory_space=pltpu.SMEM)


def params(mib):
    return pltpu.CompilerParams(
        dimension_semantics=("arbitrary",), vmem_limit_bytes=mib * 1024 * 1024
    )


def moments_kernel(charges, basis, child, parent, send, box):
    step = pl.program_id(0)
    leaf_pairs = 8 * pl.num_programs(0)
    rank = basis.shape[1]
    pairs = [
        jnp.concatenate(
            [mm(charges[c], basis[c], NT), mm(charges[c + 1], basis[c + 1], NT)], axis=1
        ).astype(bf16)
        for c in range(0, 16, 2)
    ]
    parents = [
        mm(
            jnp.concatenate(pairs[4 * p : 4 * p + 4], axis=1),
            child[8 * p : 8 * p + 8].reshape(8 * rank, rank),
        )
        for p in range(2)
    ]
    for i, pair in enumerate(pairs):
        send[step * 8 + i] = pair
    both = jnp.concatenate(parents, axis=1).astype(bf16)
    send[leaf_pairs + step] = both
    part = mm(both, parent[...].reshape(2 * rank, rank))

    @pl.when(step == 0)
    def _():
        box[...] = part

    @pl.when(step > 0)
    def _():
        box[...] += part


def moments_call(charges, basis, child, parent):
    leaves, columns, points = charges.shape
    rank = basis.shape[1]
    parents = parent.shape[0]
    steps = parents // 2
    pairs = leaves // 2 + parents // 2
    return pl.pallas_call(
        moments_kernel,
        grid=(steps,),
        in_specs=[
            pl.BlockSpec((16, columns, points), lambda i: (i, 0, 0)),
            pl.BlockSpec((16, rank, points), lambda i: (i, 0, 0)),
            pl.BlockSpec((16, rank, rank), lambda i: (i, 0, 0)),
            pl.BlockSpec((2, rank, rank), lambda i: (i, 0, 0)),
        ],
        out_specs=[
            pl.BlockSpec((pairs, columns, 2 * rank), lambda i: (0, 0, 0)),
            pl.BlockSpec((columns, rank), lambda i: (0, 0)),
        ],
        out_shape=[
            pltpu.HBM((pairs, columns, 2 * rank), bf16),
            jax.ShapeDtypeStruct((columns, rank), f32),
        ],
        compiler_params=params(16),
        name="moments",
    )(in_hbm(charges), in_hbm(basis), in_hbm(child), in_hbm(parent))


OPS_BLOCK = 128


def table_kernel(count, ops, *refs):
    *top, table, chain, turned = refs
    rank = ops.shape[1]
    half = rank // 2
    stride = turned.shape[0] // half
    first = pl.program_id(0) * OPS_BLOCK

    @pl.when(first == 0)
    def _():
        if not top:
            chain[...] = jnp.zeros_like(chain)
            return
        transfer, couple = top
        link = couple[...]
        chain[0] = link
        for j in range(1, chain.shape[0]):
            link = mm(mm(transfer[...], link, precision=highest), transfer[...], NT, precision=highest)
            chain[j] = link

    for k in range(half):
        both = jnp.concatenate([ops[0, k], ops[0, k + half]], axis=0).astype(f32)
        turned[k * stride : k * stride + OPS_BLOCK, :] = both.T

    def rows_of(start, stop):
        for o in range(start, stop):
            rows = turned[pl.ds(o, half, stride=stride), :]
            table[o] = jnp.concatenate([rows[:, :rank], rows[:, rank:]], axis=0).astype(bf16)

    rows_of(0, count % OPS_BLOCK)

    @pl.when(first + OPS_BLOCK <= count)
    def _():
        rows_of(count % OPS_BLOCK, OPS_BLOCK)


def table_call(ops, level, top, links):
    _, count, rank, _ = ops.shape
    return pl.pallas_call(
        functools.partial(table_kernel, count),
        grid=(pl.cdiv(count, OPS_BLOCK),),
        in_specs=[pl.BlockSpec((1, rank, rank, OPS_BLOCK), lambda i: (level, 0, 0, i))]
        + [VMEM for _ in top],
        out_specs=[pl.BlockSpec((OPS_BLOCK, rank, rank), lambda i: (i, 0, 0)), VMEM],
        out_shape=[
            pltpu.HBM((count, rank, rank), bf16),
            jax.ShapeDtypeStruct((links, rank, rank), f32),
        ],
        scratch_shapes=[pltpu.VMEM((rank // 2 * (OPS_BLOCK + 8), 2 * rank), f32)],
        compiler_params=params(16),
        name="operator_table",
    )(in_hbm(jnp.transpose(ops, (0, 2, 3, 1))), *top)


NEAR_LEAVES = 8


def near_kernel(base, near, left, own, right, blocks, far, out, sources, out_buf, halo_sems, out_sems):
    leaves = own.shape[0]
    count = blocks.shape[1]
    chunks = leaves // NEAR_LEAVES

    def store(c):
        rows = pl.ds(c * NEAR_LEAVES, NEAR_LEAVES)
        return pltpu.make_async_copy(out_buf.at[rows], out.at[rows], out_sems.at[c])

    halo = [
        pltpu.make_async_copy(ref, sources.at[pl.ds(i * leaves, leaves)], halo_sems.at[i])
        for i, ref in enumerate((left, own, right))
    ]
    for copy in halo:
        copy.start()
    for copy in halo:
        copy.wait()

    def one_chunk(c, _):
        results = []
        for i in range(NEAR_LEAVES):
            row = c * NEAR_LEAVES + i
            acc = far[row]
            for n in range(0, count, 2):
                lhs = jnp.concatenate(
                    [sources[near[n, row] - base[0]], sources[near[n + 1, row] - base[0]]], axis=1
                )
                rhs = jnp.concatenate([blocks[row, n], blocks[row, n + 1]], axis=1)
                acc = acc + mm(lhs, rhs, NT)
            results.append(acc)
        for i, acc in enumerate(results):
            out_buf[c * NEAR_LEAVES + i] = acc
        store(c).start()
        return 0

    lax.fori_loop(0, chunks, one_chunk, 0)
    for c in range(chunks):
        store(c).wait()


def near_call(base, near_rows, left, own, right, blocks, far):
    leaves, columns, points = own.shape
    chunks = leaves // NEAR_LEAVES
    return pl.pallas_call(
        near_kernel,
        in_specs=[SMEM, SMEM, HBM, HBM, HBM, VMEM, VMEM],
        out_specs=HBM,
        scratch_shapes=[
            pltpu.VMEM((3 * leaves, columns, points), bf16),
            pltpu.VMEM((leaves, columns, points), f32),
            pltpu.SemaphoreType.DMA((3,)),
            pltpu.SemaphoreType.DMA((chunks,)),
        ],
        out_shape=jax.ShapeDtypeStruct((leaves, columns, points), f32),
        compiler_params=pltpu.CompilerParams(vmem_limit_bytes=24 * 1024 * 1024),
        name="near",
    )(base, near_rows, in_hbm(left), in_hbm(own), in_hbm(right), blocks, far)


def doubled(pair, low):
    rank = pair.shape[1] // 2
    swapped = jnp.concatenate([pair[:, rank:], pair[:, :rank]], axis=1)
    return jnp.where(low, pair, swapped), jnp.where(low, swapped, pair)


def translated(acc, sources, table, lists, ops, base, at, low):
    for e in range(0, len(at), 4):
        picked = [sources[lists[at[e + i]] - base] for i in range(4)]
        lhs = jnp.concatenate(
            [jnp.where(low, picked[0], picked[1]), jnp.where(low, picked[2], picked[3])], axis=1
        )
        rhs = jnp.concatenate([table[ops[at[e + i]]] for i in range(4)], axis=0)
        acc = acc + mm(lhs, rhs)
    return acc


def far_kernel(
    base, list0, op0, list1, op1,
    left, own, right, leaf_ops, parent_ops, blocks, chain, parent, child, basis, *rest,
):
    siblings = rest[:-9]
    out, fetched, halo, leaf_sources, parent_sources, parent_locals, leaf_table, parent_table, sems = rest[-9:]
    leaves = basis.shape[0]
    parents = parent.shape[0]
    columns = own.shape[1]
    rank = own.shape[2] // 2
    low = lax.broadcasted_iota(jnp.int32, (columns, 2 * rank), 1) < rank
    copies = [
        pltpu.make_async_copy(source, target, sems.at[i])
        for i, (source, target) in enumerate(
            [
                (own, halo.at[1]),
                (left, halo.at[0]),
                (right, halo.at[2]),
                (parent_ops, parent_table),
                (leaf_ops, leaf_table),
                (blocks, fetched),
            ]
        )
    ]
    for copy in copies:
        copy.start()
    field = mm(siblings[0][...], chain[0], precision=highest)
    for j in range(1, len(siblings)):
        field = field + mm(siblings[j][...], chain[j], precision=highest)
    box_local = field.astype(bf16)
    for copy, i in zip(copies, (1, 0, 2)):
        copy.wait()
        for n in range(leaves // 2):
            a, b = doubled(halo[i, n], low)
            leaf_sources[i * leaves + 2 * n] = a
            leaf_sources[i * leaves + 2 * n + 1] = b
        for n in range(parents // 2):
            a, b = doubled(halo[i, leaves // 2 + n], low)
            parent_sources[i * parents + 2 * n] = a
            parent_sources[i * parents + 2 * n + 1] = b
    copies[3].wait()
    accs = [
        translated(
            mm(box_local, parent[q], NT), parent_sources, parent_table, list1, op1, base[1],
            [(q, e) for e in range(list1.shape[1])], low,
        )
        for q in range(parents)
    ]
    for q, acc in enumerate(accs):
        parent_locals[q] = acc.astype(bf16)
    copies[4].wait()

    def one_parent(q, _):
        parent_local = parent_locals[q]
        accs = [
            translated(
                mm(parent_local, child[q * 8 + c], NT), leaf_sources, leaf_table, list0, op0, base[0],
                [(e, q * 8 + c) for e in range(list0.shape[0])], low,
            )
            for c in range(8)
        ]
        results = [mm(acc.astype(bf16), basis[q * 8 + c]) for c, acc in enumerate(accs)]
        for c, acc in enumerate(results):
            out[q * 8 + c] = acc
        return 0

    lax.fori_loop(0, parents, one_parent, 0)
    copies[5].wait()


def far_call(base, list0, op0, list1, op1, left, own, right, leaf_ops, parent_ops, blocks, siblings, chain, parent, child, basis):
    leaves, rank, points = basis.shape
    parents = parent.shape[0]
    columns = own.shape[1]
    return pl.pallas_call(
        far_kernel,
        in_specs=[SMEM] * 5 + [HBM] * 6 + [VMEM] * (4 + len(siblings)),
        out_specs=[VMEM, VMEM],
        scratch_shapes=[
            pltpu.VMEM((3,) + own.shape, bf16),
            pltpu.VMEM((3 * leaves, columns, 2 * rank), bf16),
            pltpu.VMEM((3 * parents, columns, 2 * rank), bf16),
            pltpu.VMEM((parents, columns, rank), bf16),
            pltpu.VMEM(leaf_ops.shape, bf16),
            pltpu.VMEM(parent_ops.shape, bf16),
            pltpu.SemaphoreType.DMA((6,)),
        ],
        out_shape=[jax.ShapeDtypeStruct((leaves, columns, points), f32), pltpu.VMEM(blocks.shape, bf16)],
        compiler_params=pltpu.CompilerParams(vmem_limit_bytes=24 * 1024 * 1024),
        name="far",
    )(
        base, list0, op0, list1, op1,
        *[in_hbm(x) for x in (left, own, right, leaf_ops, parent_ops, blocks)],
        chain, parent, child, basis, *siblings,
    )


def to_right(block):
    count = lax.axis_size(AXES)
    return lax.ppermute(block, AXES, [(i, i + 1) for i in range(count - 1)])


def to_left(block):
    count = lax.axis_size(AXES)
    return lax.ppermute(block, AXES, [(i + 1, i) for i in range(count - 1)])


def from_partner(block, apart):
    count = lax.axis_size(AXES)
    return lax.ppermute(block, AXES, [(i, i ^ (1 << apart)) for i in range(count)])


def after(x, *arrived):
    for y in arrived:
        x = x + jnp.minimum(jnp.abs(y[0, 0, 0].astype(f32)), 0.0)
    return x


def local(
    charges, near_blocks, near_list, leaf_basis, child_transfer, parent_transfer, m2l_ops,
    far_list0, far_op0, far_list1, far_op1, top_transfer, top_couple,
):
    leaves = charges.shape[0]
    parents = parent_transfer.shape[0]
    device = lax.axis_index(AXES)
    base = jnp.stack([(device - 1) * leaves, (device - 1) * parents]).astype(jnp.int32)
    height = lax.axis_size(AXES).bit_length() - 1
    tie = lax.optimization_barrier
    charges_left = to_right(charges)
    send, total = moments_call(charges, leaf_basis, child_transfer, parent_transfer)
    siblings = []
    for level in range(height):
        if level == 1:
            total, ops = tie((total, m2l_ops))
            leaf_ops, token = table_call(ops, 0, (), 1)
        if level == 2:
            total, send = tie((after(total, charges_left), send))
            moments_left = to_right(send)
            moments_right = to_left(send)
        if level == 3:
            total, ops = tie((total, m2l_ops))
            parent_ops, chain = table_call(ops, 1, (top_transfer, top_couple), height)
        if level == height - 1:
            total = after(total, moments_left, moments_right)
        partner = from_partner(total, level)
        if level == 1:
            partner = after(partner, token)
        if level == 3:
            partner, chain = tie((partner, chain))
        if level == height - 1:
            partner, charges = tie((partner, charges))
            charges_right = to_left(charges)
        siblings.append(partner)
        total = total + partner
    far, blocks = far_call(
        base, far_list0.T, far_op0.T, far_list1, far_op1,
        moments_left, send, moments_right, leaf_ops, parent_ops, near_blocks, siblings,
        chain, parent_transfer, child_transfer, leaf_basis,
    )
    return near_call(base, near_list.T, charges_left, charges, charges_right, blocks, far)


def solution(mesh):
    split = P(AXES)
    placed = (split,) * 6 + (P(),) + (split,) * 4 + (P(), P())
    return jax.shard_map(local, mesh=mesh, in_specs=placed, out_specs=split, check_vma=False)
```

```python
import functools

import jax
import jax.numpy as jnp
from jax import lax
from jax.experimental import pallas as pl
from jax.experimental.pallas import tpu as pltpu
from jax.sharding import PartitionSpec as P

highest = lax.Precision.HIGHEST
AXES = ("sx", "sy")
f32 = jnp.float32
bf16 = jnp.bfloat16
NN = (((1,), (0,)), ((), ()))
NT = (((1,), (1,)), ((), ()))


def mm(a, b, dims=NN, precision=None):
    return lax.dot_general(a, b, dims, precision=precision, preferred_element_type=f32)


def in_hbm(x):
    return pltpu.with_memory_space_constraint(x, pltpu.HBM)


VMEM = pl.BlockSpec(memory_space=pltpu.VMEM)
HBM = pl.BlockSpec(memory_space=pltpu.HBM)
SMEM = pl.BlockSpec(memory_space=pltpu.SMEM)


def params(mib):
    return pltpu.CompilerParams(
        dimension_semantics=("arbitrary",), vmem_limit_bytes=mib * 1024 * 1024
    )


def moments_kernel(charges, basis, child, parent, send, box):
    step = pl.program_id(0)
    leaf_pairs = 8 * pl.num_programs(0)
    rank = basis.shape[1]
    pairs = [
        jnp.concatenate(
            [mm(charges[c], basis[c], NT), mm(charges[c + 1], basis[c + 1], NT)], axis=1
        ).astype(bf16)
        for c in range(0, 16, 2)
    ]
    parents = [
        mm(
            jnp.concatenate(pairs[4 * p : 4 * p + 4], axis=1),
            child[8 * p : 8 * p + 8].reshape(8 * rank, rank),
        )
        for p in range(2)
    ]
    for i, pair in enumerate(pairs):
        send[step * 8 + i] = pair
    both = jnp.concatenate(parents, axis=1).astype(bf16)
    send[leaf_pairs + step] = both
    part = mm(both, parent[...].reshape(2 * rank, rank))

    @pl.when(step == 0)
    def _():
        box[...] = part

    @pl.when(step > 0)
    def _():
        box[...] += part


def moments_call(charges, basis, child, parent):
    leaves, columns, points = charges.shape
    rank = basis.shape[1]
    parents = parent.shape[0]
    steps = parents // 2
    pairs = leaves // 2 + parents // 2
    return pl.pallas_call(
        moments_kernel,
        grid=(steps,),
        in_specs=[
            pl.BlockSpec((16, columns, points), lambda i: (i, 0, 0)),
            pl.BlockSpec((16, rank, points), lambda i: (i, 0, 0)),
            pl.BlockSpec((16, rank, rank), lambda i: (i, 0, 0)),
            pl.BlockSpec((2, rank, rank), lambda i: (i, 0, 0)),
        ],
        out_specs=[
            pl.BlockSpec((pairs, columns, 2 * rank), lambda i: (0, 0, 0)),
            pl.BlockSpec((columns, rank), lambda i: (0, 0)),
        ],
        out_shape=[
            pltpu.HBM((pairs, columns, 2 * rank), bf16),
            jax.ShapeDtypeStruct((columns, rank), f32),
        ],
        compiler_params=params(16),
        name="moments",
    )(in_hbm(charges), in_hbm(basis), in_hbm(child), in_hbm(parent))


OPS_BLOCK = 128


def table_kernel(level, ops, *refs):
    *top, table, chain, fetched, turned, turned_back, in_sems, out_sems = refs
    rank, _, count = fetched.shape
    half = rank // 2
    quarter = rank // 4
    stride = turned.shape[0] // half

    def fetch(i):
        rows = pl.ds(i * quarter, quarter)
        return pltpu.make_async_copy(ops.at[level, rows], fetched.at[rows], in_sems.at[i])

    for i in (0, 2, 1, 3):
        fetch(i).start()
    if top:
        transfer, couple = top
        link = couple[...]
        chain[0] = link
        for j in range(1, chain.shape[0]):
            link = mm(mm(transfer[...], link, precision=highest), transfer[...], NT, precision=highest)
            chain[j] = link
    else:
        chain[...] = jnp.zeros_like(chain)
    for part in range(2):
        fetch(part).wait()
        fetch(part + 2).wait()
        for k in range(part * quarter, (part + 1) * quarter):
            both = jnp.concatenate([fetched[k], fetched[k + half]], axis=0).astype(f32)
            turned[k * stride : k * stride + count, :] = both.T
    copies = []
    for first in range(0, count, OPS_BLOCK):
        size = min(OPS_BLOCK, count - first)
        for o in range(first, first + size):
            rows = turned[pl.ds(o, half, stride=stride), :]
            turned_back[o] = jnp.concatenate([rows[:, :rank], rows[:, rank:]], axis=0).astype(bf16)
        block = pl.ds(first, size)
        copies.append(
            pltpu.make_async_copy(turned_back.at[block], table.at[block], out_sems.at[first // OPS_BLOCK])
        )
        copies[-1].start()
    for copy in copies:
        copy.wait()


def table_call(ops, level, top, links):
    _, count, rank, _ = ops.shape
    stride = pl.cdiv(count, 8) * 8
    stride += 8 * (stride // 8 % 2 == 0)
    return pl.pallas_call(
        functools.partial(table_kernel, level),
        in_specs=[HBM] + [VMEM for _ in top],
        out_specs=[HBM, VMEM],
        out_shape=[
            pltpu.HBM((count, rank, rank), bf16),
            jax.ShapeDtypeStruct((links, rank, rank), f32),
        ],
        scratch_shapes=[
            pltpu.VMEM((rank, rank, count), bf16),
            pltpu.VMEM((rank // 2 * stride, 2 * rank), f32),
            pltpu.VMEM((count, rank, rank), bf16),
            pltpu.SemaphoreType.DMA((4,)),
            pltpu.SemaphoreType.DMA((pl.cdiv(count, OPS_BLOCK),)),
        ],
        compiler_params=pltpu.CompilerParams(vmem_limit_bytes=24 * 1024 * 1024),
        name="operator_table",
    )(in_hbm(jnp.transpose(ops, (0, 2, 3, 1))), *top)


NEAR_LEAVES = 8


def near_kernel(base, near, left, own, right, blocks, far, out, sources, out_buf, halo_sems, out_sems):
    leaves = own.shape[0]
    count = blocks.shape[1]
    chunks = leaves // NEAR_LEAVES

    def store(c):
        rows = pl.ds(c * NEAR_LEAVES, NEAR_LEAVES)
        return pltpu.make_async_copy(out_buf.at[rows], out.at[rows], out_sems.at[c])

    halo = [
        pltpu.make_async_copy(ref, sources.at[pl.ds(i * leaves, leaves)], halo_sems.at[i])
        for i, ref in enumerate((left, own, right))
    ]
    for copy in halo:
        copy.start()
    for copy in halo:
        copy.wait()

    def one_chunk(c, _):
        results = []
        for i in range(NEAR_LEAVES):
            row = c * NEAR_LEAVES + i
            acc = far[row]
            for n in range(0, count, 2):
                lhs = jnp.concatenate(
                    [sources[near[n, row] - base[0]], sources[near[n + 1, row] - base[0]]], axis=1
                )
                rhs = jnp.concatenate([blocks[row, n], blocks[row, n + 1]], axis=1)
                acc = acc + mm(lhs, rhs, NT)
            results.append(acc)
        for i, acc in enumerate(results):
            out_buf[c * NEAR_LEAVES + i] = acc
        store(c).start()
        return 0

    lax.fori_loop(0, chunks, one_chunk, 0)
    for c in range(chunks):
        store(c).wait()


def near_call(base, near_rows, left, own, right, blocks, far):
    leaves, columns, points = own.shape
    chunks = leaves // NEAR_LEAVES
    return pl.pallas_call(
        near_kernel,
        in_specs=[SMEM, SMEM, HBM, HBM, HBM, VMEM, VMEM],
        out_specs=HBM,
        scratch_shapes=[
            pltpu.VMEM((3 * leaves, columns, points), bf16),
            pltpu.VMEM((leaves, columns, points), f32),
            pltpu.SemaphoreType.DMA((3,)),
            pltpu.SemaphoreType.DMA((chunks,)),
        ],
        out_shape=jax.ShapeDtypeStruct((leaves, columns, points), f32),
        compiler_params=pltpu.CompilerParams(vmem_limit_bytes=24 * 1024 * 1024),
        name="near",
    )(base, near_rows, in_hbm(left), in_hbm(own), in_hbm(right), blocks, far)


def doubled(pair, low):
    rank = pair.shape[1] // 2
    swapped = jnp.concatenate([pair[:, rank:], pair[:, :rank]], axis=1)
    return jnp.where(low, pair, swapped), jnp.where(low, swapped, pair)


def translated(acc, sources, table, lists, ops, base, at, low):
    for e in range(0, len(at), 4):
        picked = [sources[lists[at[e + i]] - base] for i in range(4)]
        lhs = jnp.concatenate(
            [jnp.where(low, picked[0], picked[1]), jnp.where(low, picked[2], picked[3])], axis=1
        )
        rhs = jnp.concatenate([table[ops[at[e + i]]] for i in range(4)], axis=0)
        acc = acc + mm(lhs, rhs)
    return acc


def far_kernel(
    base, list0, op0, list1, op1,
    left, own, right, leaf_ops, parent_ops, blocks, chain, parent, child, basis, *rest,
):
    siblings = rest[:-9]
    out, fetched, halo, leaf_sources, parent_sources, parent_locals, leaf_table, parent_table, sems = rest[-9:]
    leaves = basis.shape[0]
    parents = parent.shape[0]
    columns = own.shape[1]
    rank = own.shape[2] // 2
    low = lax.broadcasted_iota(jnp.int32, (columns, 2 * rank), 1) < rank
    copies = [
        pltpu.make_async_copy(source, target, sems.at[i])
        for i, (source, target) in enumerate(
            [
                (own, halo.at[1]),
                (left, halo.at[0]),
                (right, halo.at[2]),
                (parent_ops, parent_table),
                (leaf_ops, leaf_table),
                (blocks, fetched),
            ]
        )
    ]
    for copy in copies[:5]:
        copy.start()
    field = mm(siblings[0][...], chain[0], precision=highest)
    for j in range(1, len(siblings)):
        field = field + mm(siblings[j][...], chain[j], precision=highest)
    box_local = field.astype(bf16)
    for copy, i in zip(copies, (1, 0, 2)):
        copy.wait()
        for n in range(leaves // 2):
            a, b = doubled(halo[i, n], low)
            leaf_sources[i * leaves + 2 * n] = a
            leaf_sources[i * leaves + 2 * n + 1] = b
        for n in range(parents // 2):
            a, b = doubled(halo[i, leaves // 2 + n], low)
            parent_sources[i * parents + 2 * n] = a
            parent_sources[i * parents + 2 * n + 1] = b
    copies[3].wait()
    accs = [
        translated(
            mm(box_local, parent[q], NT), parent_sources, parent_table, list1, op1, base[1],
            [(q, e) for e in range(list1.shape[1])], low,
        )
        for q in range(parents)
    ]
    for q, acc in enumerate(accs):
        parent_locals[q] = acc.astype(bf16)
    copies[4].wait()
    copies[5].start()

    def one_parent(q, _):
        parent_local = parent_locals[q]
        accs = [
            translated(
                mm(parent_local, child[q * 8 + c], NT), leaf_sources, leaf_table, list0, op0, base[0],
                [(e, q * 8 + c) for e in range(list0.shape[0])], low,
            )
            for c in range(8)
        ]
        results = [mm(acc.astype(bf16), basis[q * 8 + c]) for c, acc in enumerate(accs)]
        for c, acc in enumerate(results):
            out[q * 8 + c] = acc
        return 0

    lax.fori_loop(0, parents, one_parent, 0)
    copies[5].wait()


def far_call(base, list0, op0, list1, op1, left, own, right, leaf_ops, parent_ops, blocks, siblings, chain, parent, child, basis):
    leaves, rank, points = basis.shape
    parents = parent.shape[0]
    columns = own.shape[1]
    return pl.pallas_call(
        far_kernel,
        in_specs=[SMEM] * 5 + [HBM] * 6 + [VMEM] * (4 + len(siblings)),
        out_specs=[VMEM, VMEM],
        scratch_shapes=[
            pltpu.VMEM((3,) + own.shape, bf16),
            pltpu.VMEM((3 * leaves, columns, 2 * rank), bf16),
            pltpu.VMEM((3 * parents, columns, 2 * rank), bf16),
            pltpu.VMEM((parents, columns, rank), bf16),
            pltpu.VMEM(leaf_ops.shape, bf16),
            pltpu.VMEM(parent_ops.shape, bf16),
            pltpu.SemaphoreType.DMA((6,)),
        ],
        out_shape=[jax.ShapeDtypeStruct((leaves, columns, points), f32), pltpu.VMEM(blocks.shape, bf16)],
        compiler_params=pltpu.CompilerParams(vmem_limit_bytes=24 * 1024 * 1024),
        name="far",
    )(
        base, list0, op0, list1, op1,
        *[in_hbm(x) for x in (left, own, right, leaf_ops, parent_ops, blocks)],
        chain, parent, child, basis, *siblings,
    )


def to_right(block):
    count = lax.axis_size(AXES)
    return lax.ppermute(block, AXES, [(i, i + 1) for i in range(count - 1)])


def to_left(block):
    count = lax.axis_size(AXES)
    return lax.ppermute(block, AXES, [(i + 1, i) for i in range(count - 1)])


def from_partner(block, apart):
    count = lax.axis_size(AXES)
    return lax.ppermute(block, AXES, [(i, i ^ (1 << apart)) for i in range(count)])


def after(x, *arrived):
    for y in arrived:
        x = x + jnp.minimum(jnp.abs(y[0, : x.shape[0], : x.shape[1]].astype(f32)), 0.0)
    return x


def local(
    charges, near_blocks, near_list, leaf_basis, child_transfer, parent_transfer, m2l_ops,
    far_list0, far_op0, far_list1, far_op1, top_transfer, top_couple,
):
    leaves = charges.shape[0]
    parents = parent_transfer.shape[0]
    device = lax.axis_index(AXES)
    base = jnp.stack([(device - 1) * leaves, (device - 1) * parents]).astype(jnp.int32)
    height = lax.axis_size(AXES).bit_length() - 1
    tie = lax.optimization_barrier
    charges_left = to_right(charges)
    send, total = moments_call(charges, leaf_basis, child_transfer, parent_transfer)
    siblings = []
    for level in range(height):
        if level == 1:
            total, ops = tie((total, m2l_ops))
            leaf_ops, token = table_call(ops, 0, (), 1)
        if level == 2:
            total = after(total, charges_left)
        if level == 3:
            total, send, ops = tie((total, send, m2l_ops))
            moments_left = to_right(send)
            moments_right = to_left(send)
            parent_ops, chain = table_call(ops, 1, (top_transfer, top_couple), height)
        if level == height - 1:
            total = after(total, moments_left, moments_right)
        partner = from_partner(total, level)
        if level == 1:
            partner = after(partner, token)
        if level == 3:
            partner, chain = tie((partner, chain))
        if level == height - 1:
            partner, charges = tie((partner, charges))
            charges_right = to_left(charges)
        siblings.append(partner)
        total = total + partner
    far, blocks = far_call(
        base, far_list0.T, far_op0.T, far_list1, far_op1,
        moments_left, send, moments_right, leaf_ops, parent_ops, near_blocks, siblings,
        chain, parent_transfer, child_transfer, leaf_basis,
    )
    return near_call(base, near_list.T, charges_left, charges, charges_right, blocks, far)


def solution(mesh):
    split = P(AXES)
    placed = (split,) * 6 + (P(),) + (split,) * 4 + (P(), P())
    return jax.shard_map(local, mesh=mesh, in_specs=placed, out_specs=split, check_vma=False)
```

```python
import functools

import jax
import jax.numpy as jnp
from jax import lax
from jax.experimental import pallas as pl
from jax.experimental.pallas import tpu as pltpu
from jax.sharding import PartitionSpec as P

highest = lax.Precision.HIGHEST
AXES = ("sx", "sy")
f32 = jnp.float32
bf16 = jnp.bfloat16
NN = (((1,), (0,)), ((), ()))
NT = (((1,), (1,)), ((), ()))


def mm(a, b, dims=NN, precision=None):
    return lax.dot_general(a, b, dims, precision=precision, preferred_element_type=f32)


def in_hbm(x):
    return pltpu.with_memory_space_constraint(x, pltpu.HBM)


VMEM = pl.BlockSpec(memory_space=pltpu.VMEM)
HBM = pl.BlockSpec(memory_space=pltpu.HBM)
SMEM = pl.BlockSpec(memory_space=pltpu.SMEM)


def params(mib):
    return pltpu.CompilerParams(
        dimension_semantics=("arbitrary",), vmem_limit_bytes=mib * 1024 * 1024
    )


def moments_kernel(charges, basis, child, parent, send, box):
    step = pl.program_id(0)
    leaf_pairs = 8 * pl.num_programs(0)
    rank = basis.shape[1]
    pairs = [
        jnp.concatenate(
            [mm(charges[c], basis[c], NT), mm(charges[c + 1], basis[c + 1], NT)], axis=1
        ).astype(bf16)
        for c in range(0, 16, 2)
    ]
    parents = [
        mm(
            jnp.concatenate(pairs[4 * p : 4 * p + 4], axis=1),
            child[8 * p : 8 * p + 8].reshape(8 * rank, rank),
        )
        for p in range(2)
    ]
    for i, pair in enumerate(pairs):
        send[step * 8 + i] = pair
    both = jnp.concatenate(parents, axis=1).astype(bf16)
    send[leaf_pairs + step] = both
    part = mm(both, parent[...].reshape(2 * rank, rank))

    @pl.when(step == 0)
    def _():
        box[...] = part

    @pl.when(step > 0)
    def _():
        box[...] += part


def moments_call(charges, basis, child, parent):
    leaves, columns, points = charges.shape
    rank = basis.shape[1]
    parents = parent.shape[0]
    steps = parents // 2
    pairs = leaves // 2 + parents // 2
    return pl.pallas_call(
        moments_kernel,
        grid=(steps,),
        in_specs=[
            pl.BlockSpec((16, columns, points), lambda i: (i, 0, 0)),
            pl.BlockSpec((16, rank, points), lambda i: (i, 0, 0)),
            pl.BlockSpec((16, rank, rank), lambda i: (i, 0, 0)),
            pl.BlockSpec((2, rank, rank), lambda i: (i, 0, 0)),
        ],
        out_specs=[
            pl.BlockSpec((pairs, columns, 2 * rank), lambda i: (0, 0, 0)),
            pl.BlockSpec((columns, rank), lambda i: (0, 0)),
        ],
        out_shape=[
            pltpu.HBM((pairs, columns, 2 * rank), bf16),
            jax.ShapeDtypeStruct((columns, rank), f32),
        ],
        compiler_params=params(16),
        name="moments",
    )(in_hbm(charges), in_hbm(basis), in_hbm(child), in_hbm(parent))


OPS_BLOCK = 128


def table_kernel(level, ops, *refs):
    *top, table, chain, fetched, turned, turned_back, in_sems, out_sems = refs
    rank, _, count = fetched.shape
    half = rank // 2
    quarter = rank // 4
    stride = turned.shape[0] // half

    def fetch(i):
        rows = pl.ds(i * quarter, quarter)
        return pltpu.make_async_copy(ops.at[level, rows], fetched.at[rows], in_sems.at[i])

    for i in (0, 2, 1, 3):
        fetch(i).start()
    if top:
        transfer, couple = top
        link = couple[...]
        chain[0] = link
        for j in range(1, chain.shape[0]):
            link = mm(mm(transfer[...], link, precision=highest), transfer[...], NT, precision=highest)
            chain[j] = link
    else:
        chain[...] = jnp.zeros_like(chain)
    for part in range(2):
        fetch(part).wait()
        fetch(part + 2).wait()
        for k in range(part * quarter, (part + 1) * quarter):
            both = jnp.concatenate([fetched[k], fetched[k + half]], axis=0).astype(f32)
            turned[k * stride : k * stride + count, :] = both.T
    copies = []
    for first in range(0, count, OPS_BLOCK):
        size = min(OPS_BLOCK, count - first)
        for o in range(first, first + size):
            rows = turned[pl.ds(o, half, stride=stride), :]
            turned_back[o] = jnp.concatenate([rows[:, :rank], rows[:, rank:]], axis=0).astype(bf16)
        block = pl.ds(first, size)
        copies.append(
            pltpu.make_async_copy(turned_back.at[block], table.at[block], out_sems.at[first // OPS_BLOCK])
        )
        copies[-1].start()
    for copy in copies:
        copy.wait()


def table_call(ops, level, top, links):
    _, count, rank, _ = ops.shape
    stride = pl.cdiv(count, 8) * 8
    stride += 8 * (stride // 8 % 2 == 0)
    return pl.pallas_call(
        functools.partial(table_kernel, level),
        in_specs=[HBM] + [VMEM for _ in top],
        out_specs=[HBM, VMEM],
        out_shape=[
            pltpu.HBM((count, rank, rank), bf16),
            jax.ShapeDtypeStruct((links, rank, rank), f32),
        ],
        scratch_shapes=[
            pltpu.VMEM((rank, rank, count), bf16),
            pltpu.VMEM((rank // 2 * stride, 2 * rank), f32),
            pltpu.VMEM((count, rank, rank), bf16),
            pltpu.SemaphoreType.DMA((4,)),
            pltpu.SemaphoreType.DMA((pl.cdiv(count, OPS_BLOCK),)),
        ],
        compiler_params=pltpu.CompilerParams(vmem_limit_bytes=24 * 1024 * 1024),
        name="operator_table",
    )(in_hbm(jnp.transpose(ops, (0, 2, 3, 1))), *top)


NEAR_LEAVES = 16


def near_kernel(base, near, left, own, right, blocks, far, out, sources, out_buf, halo_sems, out_sems):
    leaves = own.shape[0]
    count = blocks.shape[1]
    chunks = leaves // NEAR_LEAVES

    def store(c):
        rows = pl.ds(c * NEAR_LEAVES, NEAR_LEAVES)
        return pltpu.make_async_copy(out_buf.at[rows], out.at[rows], out_sems.at[c])

    halo = [
        pltpu.make_async_copy(ref, sources.at[pl.ds(i * leaves, leaves)], halo_sems.at[i])
        for i, ref in enumerate((left, own, right))
    ]
    for copy in halo:
        copy.start()
    for copy in halo:
        copy.wait()

    def one_chunk(c, _):
        results = []
        for i in range(NEAR_LEAVES):
            row = c * NEAR_LEAVES + i
            acc = None
            for n in range(0, count, 2):
                lhs = jnp.concatenate([blocks[row, n], blocks[row, n + 1]], axis=1)
                rhs = jnp.concatenate(
                    [sources[near[n, row] - base[0]], sources[near[n + 1, row] - base[0]]], axis=1
                )
                term = mm(lhs, rhs, NT)
                acc = term if acc is None else acc + term
            results.append(far[row] + acc.T)
        for i, acc in enumerate(results):
            out_buf[c * NEAR_LEAVES + i] = acc
        store(c).start()
        return 0

    lax.fori_loop(0, chunks, one_chunk, 0)
    for c in range(chunks):
        store(c).wait()


def near_call(base, near_rows, left, own, right, blocks, far):
    leaves, columns, points = own.shape
    chunks = leaves // NEAR_LEAVES
    return pl.pallas_call(
        near_kernel,
        in_specs=[SMEM, SMEM, HBM, HBM, HBM, VMEM, VMEM],
        out_specs=HBM,
        scratch_shapes=[
            pltpu.VMEM((3 * leaves, columns, points), bf16),
            pltpu.VMEM((leaves, columns, points), f32),
            pltpu.SemaphoreType.DMA((3,)),
            pltpu.SemaphoreType.DMA((chunks,)),
        ],
        out_shape=jax.ShapeDtypeStruct((leaves, columns, points), f32),
        compiler_params=pltpu.CompilerParams(vmem_limit_bytes=24 * 1024 * 1024),
        name="near",
    )(base, near_rows, in_hbm(left), in_hbm(own), in_hbm(right), blocks, far)


def doubled(pair, low):
    rank = pair.shape[1] // 2
    swapped = jnp.concatenate([pair[:, rank:], pair[:, :rank]], axis=1)
    return jnp.where(low, pair, swapped), jnp.where(low, swapped, pair)


def translated(acc, sources, table, lists, ops, base, at, low):
    for e in range(0, len(at), 4):
        picked = [sources[lists[at[e + i]] - base] for i in range(4)]
        lhs = jnp.concatenate(
            [jnp.where(low, picked[0], picked[1]), jnp.where(low, picked[2], picked[3])], axis=1
        )
        rhs = jnp.concatenate([table[ops[at[e + i]]] for i in range(4)], axis=0)
        acc = acc + mm(lhs, rhs)
    return acc


def far_kernel(
    base, list0, op0, list1, op1,
    left, own, right, leaf_ops, parent_ops, blocks, chain, parent, child, basis, *rest,
):
    siblings = rest[:-9]
    out, fetched, halo, leaf_sources, parent_sources, parent_locals, leaf_table, parent_table, sems = rest[-9:]
    leaves = basis.shape[0]
    parents = parent.shape[0]
    columns = own.shape[1]
    rank = own.shape[2] // 2
    low = lax.broadcasted_iota(jnp.int32, (columns, 2 * rank), 1) < rank
    copies = [
        pltpu.make_async_copy(source, target, sems.at[i])
        for i, (source, target) in enumerate(
            [
                (own, halo.at[1]),
                (left, halo.at[0]),
                (right, halo.at[2]),
                (parent_ops, parent_table),
                (leaf_ops, leaf_table),
                (blocks, fetched),
            ]
        )
    ]
    for copy in copies[:5]:
        copy.start()
    field = mm(siblings[0][...], chain[0], precision=highest)
    for j in range(1, len(siblings)):
        field = field + mm(siblings[j][...], chain[j], precision=highest)
    box_local = field.astype(bf16)
    for copy, i in zip(copies, (1, 0, 2)):
        copy.wait()
        for n in range(leaves // 2):
            a, b = doubled(halo[i, n], low)
            leaf_sources[i * leaves + 2 * n] = a
            leaf_sources[i * leaves + 2 * n + 1] = b
        for n in range(parents // 2):
            a, b = doubled(halo[i, leaves // 2 + n], low)
            parent_sources[i * parents + 2 * n] = a
            parent_sources[i * parents + 2 * n + 1] = b
    copies[3].wait()
    accs = [
        translated(
            mm(box_local, parent[q], NT), parent_sources, parent_table, list1, op1, base[1],
            [(q, e) for e in range(list1.shape[1])], low,
        )
        for q in range(parents)
    ]
    for q, acc in enumerate(accs):
        parent_locals[q] = acc.astype(bf16)
    copies[4].wait()
    copies[5].start()

    def one_parent(q, _):
        parent_local = parent_locals[q]
        accs = [
            translated(
                mm(parent_local, child[q * 8 + c], NT), leaf_sources, leaf_table, list0, op0, base[0],
                [(e, q * 8 + c) for e in range(list0.shape[0])], low,
            )
            for c in range(8)
        ]
        results = [mm(acc.astype(bf16), basis[q * 8 + c]) for c, acc in enumerate(accs)]
        for c, acc in enumerate(results):
            out[q * 8 + c] = acc
        return 0

    lax.fori_loop(0, parents, one_parent, 0)
    copies[5].wait()


def far_call(base, list0, op0, list1, op1, left, own, right, leaf_ops, parent_ops, blocks, siblings, chain, parent, child, basis):
    leaves, rank, points = basis.shape
    parents = parent.shape[0]
    columns = own.shape[1]
    return pl.pallas_call(
        far_kernel,
        in_specs=[SMEM] * 5 + [HBM] * 6 + [VMEM] * (4 + len(siblings)),
        out_specs=[VMEM, VMEM],
        scratch_shapes=[
            pltpu.VMEM((3,) + own.shape, bf16),
            pltpu.VMEM((3 * leaves, columns, 2 * rank), bf16),
            pltpu.VMEM((3 * parents, columns, 2 * rank), bf16),
            pltpu.VMEM((parents, columns, rank), bf16),
            pltpu.VMEM(leaf_ops.shape, bf16),
            pltpu.VMEM(parent_ops.shape, bf16),
            pltpu.SemaphoreType.DMA((6,)),
        ],
        out_shape=[jax.ShapeDtypeStruct((leaves, columns, points), f32), pltpu.VMEM(blocks.shape, bf16)],
        compiler_params=pltpu.CompilerParams(vmem_limit_bytes=24 * 1024 * 1024),
        name="far",
    )(
        base, list0, op0, list1, op1,
        *[in_hbm(x) for x in (left, own, right, leaf_ops, parent_ops, blocks)],
        chain, parent, child, basis, *siblings,
    )


def to_right(block):
    count = lax.axis_size(AXES)
    return lax.ppermute(block, AXES, [(i, i + 1) for i in range(count - 1)])


def to_left(block):
    count = lax.axis_size(AXES)
    return lax.ppermute(block, AXES, [(i + 1, i) for i in range(count - 1)])


def from_partner(block, apart):
    count = lax.axis_size(AXES)
    return lax.ppermute(block, AXES, [(i, i ^ (1 << apart)) for i in range(count)])


def after(x, *arrived):
    for y in arrived:
        x = x + jnp.minimum(jnp.abs(y[0, : x.shape[0], : x.shape[1]].astype(f32)), 0.0)
    return x


def local(
    charges, near_blocks, near_list, leaf_basis, child_transfer, parent_transfer, m2l_ops,
    far_list0, far_op0, far_list1, far_op1, top_transfer, top_couple,
):
    leaves = charges.shape[0]
    parents = parent_transfer.shape[0]
    device = lax.axis_index(AXES)
    base = jnp.stack([(device - 1) * leaves, (device - 1) * parents]).astype(jnp.int32)
    height = lax.axis_size(AXES).bit_length() - 1
    tie = lax.optimization_barrier
    charges_left = to_right(charges)
    send, total = moments_call(charges, leaf_basis, child_transfer, parent_transfer)
    siblings = []
    for level in range(height):
        if level == 1:
            total, ops = tie((total, m2l_ops))
            leaf_ops, token = table_call(ops, 0, (), 1)
        if level == 2:
            total = after(total, charges_left)
        if level == 3:
            total, send, ops = tie((total, send, m2l_ops))
            moments_left = to_right(send)
            moments_right = to_left(send)
            parent_ops, chain = table_call(ops, 1, (top_transfer, top_couple), height)
        partner = from_partner(total, level)
        if level == 1:
            partner = after(partner, token)
        if level == 3:
            partner, chain = tie((partner, chain))
        if level == height - 1:
            partner, charges, moments_left, moments_right = tie(
                (partner, charges, moments_left, moments_right)
            )
            charges_right = to_left(charges)
        siblings.append(partner)
        total = total + partner
    far, blocks = far_call(
        base, far_list0.T, far_op0.T, far_list1, far_op1,
        moments_left, send, moments_right, leaf_ops, parent_ops, near_blocks, siblings,
        chain, parent_transfer, child_transfer, leaf_basis,
    )
    return near_call(base, near_list.T, charges_left, charges, charges_right, blocks, far)


def solution(mesh):
    split = P(AXES)
    placed = (split,) * 6 + (P(),) + (split,) * 4 + (P(), P())
    return jax.shard_map(local, mesh=mesh, in_specs=placed, out_specs=split, check_vma=False)
```

```python
import functools

import jax
import jax.numpy as jnp
from jax import lax
from jax.experimental import pallas as pl
from jax.experimental.pallas import tpu as pltpu
from jax.sharding import PartitionSpec as P

highest = lax.Precision.HIGHEST
AXES = ("sx", "sy")
f32 = jnp.float32
bf16 = jnp.bfloat16
NN = (((1,), (0,)), ((), ()))
NT = (((1,), (1,)), ((), ()))


def mm(a, b, dims=NN, precision=None):
    return lax.dot_general(a, b, dims, precision=precision, preferred_element_type=f32)


def in_hbm(x):
    return pltpu.with_memory_space_constraint(x, pltpu.HBM)


VMEM = pl.BlockSpec(memory_space=pltpu.VMEM)
HBM = pl.BlockSpec(memory_space=pltpu.HBM)
SMEM = pl.BlockSpec(memory_space=pltpu.SMEM)


def params(mib):
    return pltpu.CompilerParams(
        dimension_semantics=("arbitrary",), vmem_limit_bytes=mib * 1024 * 1024
    )


def moments_kernel(charges, basis, child, parent, send, box):
    step = pl.program_id(0)
    leaf_pairs = 8 * pl.num_programs(0)
    rank = basis.shape[1]
    pairs = [
        jnp.concatenate(
            [mm(charges[c], basis[c], NT), mm(charges[c + 1], basis[c + 1], NT)], axis=1
        ).astype(bf16)
        for c in range(0, 16, 2)
    ]
    parents = [
        mm(
            jnp.concatenate(pairs[4 * p : 4 * p + 4], axis=1),
            child[8 * p : 8 * p + 8].reshape(8 * rank, rank),
        )
        for p in range(2)
    ]
    for i, pair in enumerate(pairs):
        send[step * 8 + i] = pair
    both = jnp.concatenate(parents, axis=1).astype(bf16)
    send[leaf_pairs + step] = both
    part = mm(both, parent[...].reshape(2 * rank, rank))

    @pl.when(step == 0)
    def _():
        box[...] = part

    @pl.when(step > 0)
    def _():
        box[...] += part


def moments_call(charges, basis, child, parent):
    leaves, columns, points = charges.shape
    rank = basis.shape[1]
    parents = parent.shape[0]
    steps = parents // 2
    pairs = leaves // 2 + parents // 2
    return pl.pallas_call(
        moments_kernel,
        grid=(steps,),
        in_specs=[
            pl.BlockSpec((16, columns, points), lambda i: (i, 0, 0)),
            pl.BlockSpec((16, rank, points), lambda i: (i, 0, 0)),
            pl.BlockSpec((16, rank, rank), lambda i: (i, 0, 0)),
            pl.BlockSpec((2, rank, rank), lambda i: (i, 0, 0)),
        ],
        out_specs=[
            pl.BlockSpec((pairs, columns, 2 * rank), lambda i: (0, 0, 0)),
            pl.BlockSpec((columns, rank), lambda i: (0, 0)),
        ],
        out_shape=[
            pltpu.HBM((pairs, columns, 2 * rank), bf16),
            jax.ShapeDtypeStruct((columns, rank), f32),
        ],
        compiler_params=params(16),
        name="moments",
    )(in_hbm(charges), in_hbm(basis), in_hbm(child), in_hbm(parent))


OPS_BLOCK = 128


def table_kernel(level, ops, *refs):
    *top, table, chain, fetched, turned, turned_back, in_sems, out_sems = refs
    rank, _, count = fetched.shape
    half = rank // 2
    quarter = rank // 4
    stride = turned.shape[0] // half

    def fetch(i):
        rows = pl.ds(i * quarter, quarter)
        return pltpu.make_async_copy(ops.at[level, rows], fetched.at[rows], in_sems.at[i])

    for i in (0, 2, 1, 3):
        fetch(i).start()
    if top:
        transfer, couple = top
        link = couple[...]
        chain[0] = link
        for j in range(1, chain.shape[0]):
            link = mm(mm(transfer[...], link, precision=highest), transfer[...], NT, precision=highest)
            chain[j] = link
    else:
        chain[...] = jnp.zeros_like(chain)
    for part in range(2):
        fetch(part).wait()
        fetch(part + 2).wait()
        for k in range(part * quarter, (part + 1) * quarter):
            both = jnp.concatenate([fetched[k], fetched[k + half]], axis=0).astype(f32)
            turned[k * stride : k * stride + count, :] = both.T
    copies = []
    for first in range(0, count, OPS_BLOCK):
        size = min(OPS_BLOCK, count - first)
        for o in range(first, first + size):
            rows = turned[pl.ds(o, half, stride=stride), :]
            turned_back[o] = jnp.concatenate([rows[:, :rank], rows[:, rank:]], axis=0).astype(bf16)
        block = pl.ds(first, size)
        copies.append(
            pltpu.make_async_copy(turned_back.at[block], table.at[block], out_sems.at[first // OPS_BLOCK])
        )
        copies[-1].start()
    for copy in copies:
        copy.wait()


def table_call(ops, level, top, links):
    _, count, rank, _ = ops.shape
    stride = pl.cdiv(count, 8) * 8
    stride += 8 * (stride // 8 % 2 == 0)
    return pl.pallas_call(
        functools.partial(table_kernel, level),
        in_specs=[HBM] + [VMEM for _ in top],
        out_specs=[HBM, VMEM],
        out_shape=[
            pltpu.HBM((count, rank, rank), bf16),
            jax.ShapeDtypeStruct((links, rank, rank), f32),
        ],
        scratch_shapes=[
            pltpu.VMEM((rank, rank, count), bf16),
            pltpu.VMEM((rank // 2 * stride, 2 * rank), f32),
            pltpu.VMEM((count, rank, rank), bf16),
            pltpu.SemaphoreType.DMA((4,)),
            pltpu.SemaphoreType.DMA((pl.cdiv(count, OPS_BLOCK),)),
        ],
        compiler_params=pltpu.CompilerParams(vmem_limit_bytes=24 * 1024 * 1024),
        name="operator_table",
    )(in_hbm(jnp.transpose(ops, (0, 2, 3, 1))), *top)


NEAR_LEAVES = 16


def near_kernel(base, near, left, own, right, blocks, far, out, sources, out_buf, halo_sems, out_sems):
    leaves = own.shape[0]
    count = blocks.shape[1]
    chunks = leaves // NEAR_LEAVES

    def store(c):
        rows = pl.ds(c * NEAR_LEAVES, NEAR_LEAVES)
        return pltpu.make_async_copy(out_buf.at[rows], out.at[rows], out_sems.at[c])

    halo = [
        pltpu.make_async_copy(ref, sources.at[pl.ds(i * leaves, leaves)], halo_sems.at[i])
        for i, ref in enumerate((left, own, right))
    ]
    for copy in halo:
        copy.start()
    for copy in halo:
        copy.wait()

    def one_chunk(c, _):
        results = []
        for i in range(NEAR_LEAVES):
            row = c * NEAR_LEAVES + i
            acc = None
            for n in range(0, count, 2):
                lhs = jnp.concatenate([blocks[row, n], blocks[row, n + 1]], axis=1)
                rhs = jnp.concatenate(
                    [sources[near[n, row] - base[0]], sources[near[n + 1, row] - base[0]]], axis=1
                )
                term = mm(lhs, rhs, NT)
                acc = term if acc is None else acc + term
            results.append(far[row] + acc.T)
        for i, acc in enumerate(results):
            out_buf[c * NEAR_LEAVES + i] = acc
        store(c).start()
        return 0

    lax.fori_loop(0, chunks, one_chunk, 0)
    for c in range(chunks):
        store(c).wait()


def near_call(base, near_rows, left, own, right, blocks, far):
    leaves, columns, points = own.shape
    chunks = leaves // NEAR_LEAVES
    return pl.pallas_call(
        near_kernel,
        in_specs=[SMEM, SMEM, HBM, HBM, HBM, VMEM, VMEM],
        out_specs=HBM,
        scratch_shapes=[
            pltpu.VMEM((3 * leaves, columns, points), bf16),
            pltpu.VMEM((leaves, columns, points), f32),
            pltpu.SemaphoreType.DMA((3,)),
            pltpu.SemaphoreType.DMA((chunks,)),
        ],
        out_shape=jax.ShapeDtypeStruct((leaves, columns, points), f32),
        compiler_params=pltpu.CompilerParams(vmem_limit_bytes=24 * 1024 * 1024),
        name="near",
    )(base, near_rows, in_hbm(left), in_hbm(own), in_hbm(right), blocks, far)


def doubled(pair, low):
    rank = pair.shape[1] // 2
    swapped = jnp.concatenate([pair[:, rank:], pair[:, :rank]], axis=1)
    return jnp.where(low, pair, swapped), jnp.where(low, swapped, pair)


def translated(acc, sources, table, lists, ops, base, at, low):
    for e in range(0, len(at), 4):
        picked = [sources[lists[at[e + i]] - base] for i in range(4)]
        lhs = jnp.concatenate(
            [jnp.where(low, picked[0], picked[1]), jnp.where(low, picked[2], picked[3])], axis=1
        )
        rhs = jnp.concatenate([table[ops[at[e + i]]] for i in range(4)], axis=0)
        acc = acc + mm(lhs, rhs)
    return acc


def far_kernel(
    base, list0, op0, list1, op1,
    left, own, right, leaf_ops, parent_ops, blocks, chain, parent, child, basis, *rest,
):
    siblings = rest[:-9]
    out, fetched, halo, leaf_sources, parent_sources, parent_locals, leaf_table, parent_table, sems = rest[-9:]
    leaves = basis.shape[0]
    parents = parent.shape[0]
    columns = own.shape[1]
    rank = own.shape[2] // 2
    low = lax.broadcasted_iota(jnp.int32, (columns, 2 * rank), 1) < rank
    copies = [
        pltpu.make_async_copy(source, target, sems.at[i])
        for i, (source, target) in enumerate(
            [
                (own, halo.at[1]),
                (left, halo.at[0]),
                (right, halo.at[2]),
                (parent_ops, parent_table),
                (leaf_ops, leaf_table),
                (blocks, fetched),
            ]
        )
    ]
    for copy in copies[:5]:
        copy.start()
    field = mm(siblings[0][...], chain[0], precision=highest)
    for j in range(1, len(siblings)):
        field = field + mm(siblings[j][...], chain[j], precision=highest)
    box_local = field.astype(bf16)
    for copy, i in zip(copies, (1, 0, 2)):
        copy.wait()
        for n in range(leaves // 2):
            a, b = doubled(halo[i, n], low)
            leaf_sources[i * leaves + 2 * n] = a
            leaf_sources[i * leaves + 2 * n + 1] = b
        for n in range(parents // 2):
            a, b = doubled(halo[i, leaves // 2 + n], low)
            parent_sources[i * parents + 2 * n] = a
            parent_sources[i * parents + 2 * n + 1] = b
    copies[3].wait()
    accs = [
        translated(
            mm(box_local, parent[q], NT), parent_sources, parent_table, list1, op1, base[1],
            [(q, e) for e in range(list1.shape[1])], low,
        )
        for q in range(parents)
    ]
    for q, acc in enumerate(accs):
        parent_locals[q] = acc.astype(bf16)
    copies[4].wait()
    copies[5].start()

    def one_parent(q, _):
        parent_local = parent_locals[q]
        accs = [
            translated(
                mm(parent_local, child[q * 8 + c], NT), leaf_sources, leaf_table, list0, op0, base[0],
                [(e, q * 8 + c) for e in range(list0.shape[0])], low,
            )
            for c in range(8)
        ]
        results = [mm(acc.astype(bf16), basis[q * 8 + c]) for c, acc in enumerate(accs)]
        for c, acc in enumerate(results):
            out[q * 8 + c] = acc
        return 0

    lax.fori_loop(0, parents, one_parent, 0)
    copies[5].wait()


def far_call(base, list0, op0, list1, op1, left, own, right, leaf_ops, parent_ops, blocks, siblings, chain, parent, child, basis):
    leaves, rank, points = basis.shape
    parents = parent.shape[0]
    columns = own.shape[1]
    return pl.pallas_call(
        far_kernel,
        in_specs=[SMEM] * 5 + [HBM] * 6 + [VMEM] * (4 + len(siblings)),
        out_specs=[VMEM, VMEM],
        scratch_shapes=[
            pltpu.VMEM((3,) + own.shape, bf16),
            pltpu.VMEM((3 * leaves, columns, 2 * rank), bf16),
            pltpu.VMEM((3 * parents, columns, 2 * rank), bf16),
            pltpu.VMEM((parents, columns, rank), bf16),
            pltpu.VMEM(leaf_ops.shape, bf16),
            pltpu.VMEM(parent_ops.shape, bf16),
            pltpu.SemaphoreType.DMA((6,)),
        ],
        out_shape=[jax.ShapeDtypeStruct((leaves, columns, points), f32), pltpu.VMEM(blocks.shape, bf16)],
        compiler_params=pltpu.CompilerParams(vmem_limit_bytes=24 * 1024 * 1024),
        name="far",
    )(
        base, list0, op0, list1, op1,
        *[in_hbm(x) for x in (left, own, right, leaf_ops, parent_ops, blocks)],
        chain, parent, child, basis, *siblings,
    )


def to_right(block):
    count = lax.axis_size(AXES)
    return lax.ppermute(block, AXES, [(i, i + 1) for i in range(count - 1)])


def to_left(block):
    count = lax.axis_size(AXES)
    return lax.ppermute(block, AXES, [(i + 1, i) for i in range(count - 1)])


def from_partner(block, apart):
    count = lax.axis_size(AXES)
    return lax.ppermute(block, AXES, [(i, i ^ (1 << apart)) for i in range(count)])


def after(x, *arrived):
    for y in arrived:
        x = x + jnp.minimum(jnp.abs(y[0, : x.shape[0], : x.shape[1]].astype(f32)), 0.0)
    return x


def local(
    charges, near_blocks, near_list, leaf_basis, child_transfer, parent_transfer, m2l_ops,
    far_list0, far_op0, far_list1, far_op1, top_transfer, top_couple,
):
    leaves = charges.shape[0]
    parents = parent_transfer.shape[0]
    device = lax.axis_index(AXES)
    base = jnp.stack([(device - 1) * leaves, (device - 1) * parents]).astype(jnp.int32)
    height = lax.axis_size(AXES).bit_length() - 1
    tie = lax.optimization_barrier
    charges_left = to_right(charges)
    send, total = moments_call(charges, leaf_basis, child_transfer, parent_transfer)
    siblings = []
    for level in range(height):
        if level == 1:
            total, ops = tie((total, m2l_ops))
            leaf_ops, token = table_call(ops, 0, (), 1)
        if level == 2:
            total = after(total, charges_left)
        if level == 4:
            total, send, ops = tie((total, send, m2l_ops))
            moments_left = to_right(send)
            moments_right = to_left(send)
            parent_ops, chain = table_call(ops, 1, (top_transfer, top_couple), height)
        partner = from_partner(total, level)
        if level == 1:
            partner = after(partner, token)
        if level == 4:
            partner, chain = tie((partner, chain))
        if level == height - 1:
            partner, charges, moments_left, moments_right = tie(
                (partner, charges, moments_left, moments_right)
            )
            charges_right = to_left(charges)
        siblings.append(partner)
        total = total + partner
    far, blocks = far_call(
        base, far_list0.T, far_op0.T, far_list1, far_op1,
        moments_left, send, moments_right, leaf_ops, parent_ops, near_blocks, siblings,
        chain, parent_transfer, child_transfer, leaf_basis,
    )
    return near_call(base, near_list.T, charges_left, charges, charges_right, blocks, far)


def solution(mesh):
    split = P(AXES)
    placed = (split,) * 6 + (P(),) + (split,) * 4 + (P(), P())
    return jax.shard_map(local, mesh=mesh, in_specs=placed, out_specs=split, check_vma=False)
```

```python
import functools

import jax
import jax.numpy as jnp
from jax import lax
from jax.experimental import pallas as pl
from jax.experimental.pallas import tpu as pltpu
from jax.sharding import PartitionSpec as P

highest = lax.Precision.HIGHEST
AXES = ("sx", "sy")
f32 = jnp.float32
bf16 = jnp.bfloat16
NN = (((1,), (0,)), ((), ()))
NT = (((1,), (1,)), ((), ()))


def mm(a, b, dims=NN, precision=None):
    return lax.dot_general(a, b, dims, precision=precision, preferred_element_type=f32)


def in_hbm(x):
    return pltpu.with_memory_space_constraint(x, pltpu.HBM)


VMEM = pl.BlockSpec(memory_space=pltpu.VMEM)
HBM = pl.BlockSpec(memory_space=pltpu.HBM)
SMEM = pl.BlockSpec(memory_space=pltpu.SMEM)


def params(mib):
    return pltpu.CompilerParams(
        dimension_semantics=("arbitrary",), vmem_limit_bytes=mib * 1024 * 1024
    )


def moments_kernel(charges, basis, child, parent, send, box):
    step = pl.program_id(0)
    leaf_pairs = 8 * pl.num_programs(0)
    rank = basis.shape[1]
    pairs = [
        jnp.concatenate(
            [mm(charges[c], basis[c], NT), mm(charges[c + 1], basis[c + 1], NT)], axis=1
        ).astype(bf16)
        for c in range(0, 16, 2)
    ]
    parents = [
        mm(
            jnp.concatenate(pairs[4 * p : 4 * p + 4], axis=1),
            child[8 * p : 8 * p + 8].reshape(8 * rank, rank),
        )
        for p in range(2)
    ]
    for i, pair in enumerate(pairs):
        send[step * 8 + i] = pair
    both = jnp.concatenate(parents, axis=1).astype(bf16)
    send[leaf_pairs + step] = both
    part = mm(both, parent[...].reshape(2 * rank, rank))

    @pl.when(step == 0)
    def _():
        box[...] = part

    @pl.when(step > 0)
    def _():
        box[...] += part


def moments_call(charges, basis, child, parent):
    leaves, columns, points = charges.shape
    rank = basis.shape[1]
    parents = parent.shape[0]
    steps = parents // 2
    pairs = leaves // 2 + parents // 2
    return pl.pallas_call(
        moments_kernel,
        grid=(steps,),
        in_specs=[
            pl.BlockSpec((16, columns, points), lambda i: (i, 0, 0)),
            pl.BlockSpec((16, rank, points), lambda i: (i, 0, 0)),
            pl.BlockSpec((16, rank, rank), lambda i: (i, 0, 0)),
            pl.BlockSpec((2, rank, rank), lambda i: (i, 0, 0)),
        ],
        out_specs=[
            pl.BlockSpec((pairs, columns, 2 * rank), lambda i: (0, 0, 0)),
            pl.BlockSpec((columns, rank), lambda i: (0, 0)),
        ],
        out_shape=[
            pltpu.HBM((pairs, columns, 2 * rank), bf16),
            jax.ShapeDtypeStruct((columns, rank), f32),
        ],
        compiler_params=params(16),
        name="moments",
    )(in_hbm(charges), in_hbm(basis), in_hbm(child), in_hbm(parent))


OPS_BLOCK = 128


def table_kernel(level, ops, *refs):
    *top, table, chain, fetched, turned, turned_back, in_sems, out_sems = refs
    rank, _, count = fetched.shape
    half = rank // 2
    quarter = rank // 4
    stride = turned.shape[0] // half

    def fetch(i):
        rows = pl.ds(i * quarter, quarter)
        return pltpu.make_async_copy(ops.at[level, rows], fetched.at[rows], in_sems.at[i])

    for i in (0, 2, 1, 3):
        fetch(i).start()
    if top:
        transfer, couple = top
        link = couple[...]
        chain[0] = link
        for j in range(1, chain.shape[0]):
            link = mm(mm(transfer[...], link, precision=highest), transfer[...], NT, precision=highest)
            chain[j] = link
    else:
        chain[...] = jnp.zeros_like(chain)
    for part in range(2):
        fetch(part).wait()
        fetch(part + 2).wait()
        for k in range(part * quarter, (part + 1) * quarter):
            both = jnp.concatenate([fetched[k], fetched[k + half]], axis=0).astype(f32)
            turned[k * stride : k * stride + count, :] = both.T
    copies = []
    for first in range(0, count, OPS_BLOCK):
        size = min(OPS_BLOCK, count - first)
        for o in range(first, first + size):
            rows = turned[pl.ds(o, half, stride=stride), :]
            if turned_back.shape[1] == rank:
                rows = jnp.concatenate([rows[:, :rank], rows[:, rank:]], axis=0)
            turned_back[o] = rows.astype(bf16)
        block = pl.ds(first, size)
        copies.append(
            pltpu.make_async_copy(turned_back.at[block], table.at[block], out_sems.at[first // OPS_BLOCK])
        )
        copies[-1].start()
    for copy in copies:
        copy.wait()


def table_call(ops, level, packed, top, links):
    _, count, rank, _ = ops.shape
    shape = (count, rank // 2, 2 * rank) if packed else (count, rank, rank)
    stride = pl.cdiv(count, 8) * 8
    stride += 8 * (stride // 8 % 2 == 0)
    return pl.pallas_call(
        functools.partial(table_kernel, level),
        in_specs=[HBM] + [VMEM for _ in top],
        out_specs=[HBM, VMEM],
        out_shape=[
            pltpu.HBM(shape, bf16),
            jax.ShapeDtypeStruct((links, rank, rank), f32),
        ],
        scratch_shapes=[
            pltpu.VMEM((rank, rank, count), bf16),
            pltpu.VMEM((rank // 2 * stride, 2 * rank), f32),
            pltpu.VMEM(shape, bf16),
            pltpu.SemaphoreType.DMA((4,)),
            pltpu.SemaphoreType.DMA((pl.cdiv(count, OPS_BLOCK),)),
        ],
        compiler_params=pltpu.CompilerParams(vmem_limit_bytes=24 * 1024 * 1024),
        name="operator_table",
    )(in_hbm(jnp.transpose(ops, (0, 2, 3, 1))), *top)


NEAR_LEAVES = 16


def near_kernel(base, near, left, own, right, blocks, far, out, sources, out_buf, halo_sems, out_sems):
    leaves = own.shape[0]
    count = blocks.shape[1]
    chunks = leaves // NEAR_LEAVES

    def store(c):
        rows = pl.ds(c * NEAR_LEAVES, NEAR_LEAVES)
        return pltpu.make_async_copy(out_buf.at[rows], out.at[rows], out_sems.at[c])

    halo = [
        pltpu.make_async_copy(ref, sources.at[pl.ds(i * leaves, leaves)], halo_sems.at[i])
        for i, ref in enumerate((left, own, right))
    ]
    for copy in halo:
        copy.start()
    for copy in halo:
        copy.wait()

    def one_chunk(c, _):
        results = []
        for i in range(NEAR_LEAVES):
            row = c * NEAR_LEAVES + i
            acc = None
            for n in range(0, count, 2):
                lhs = jnp.concatenate([blocks[row, n], blocks[row, n + 1]], axis=1)
                rhs = jnp.concatenate(
                    [sources[near[n, row] - base[0]], sources[near[n + 1, row] - base[0]]], axis=1
                )
                term = mm(lhs, rhs, NT)
                acc = term if acc is None else acc + term
            results.append(far[row] + acc.T)
        for i, acc in enumerate(results):
            out_buf[c * NEAR_LEAVES + i] = acc
        store(c).start()
        return 0

    lax.fori_loop(0, chunks, one_chunk, 0)
    for c in range(chunks):
        store(c).wait()


def near_call(base, near_rows, left, own, right, blocks, far):
    leaves, columns, points = own.shape
    chunks = leaves // NEAR_LEAVES
    return pl.pallas_call(
        near_kernel,
        in_specs=[SMEM, SMEM, HBM, HBM, HBM, VMEM, VMEM],
        out_specs=HBM,
        scratch_shapes=[
            pltpu.VMEM((3 * leaves, columns, points), bf16),
            pltpu.VMEM((leaves, columns, points), f32),
            pltpu.SemaphoreType.DMA((3,)),
            pltpu.SemaphoreType.DMA((chunks,)),
        ],
        out_shape=jax.ShapeDtypeStruct((leaves, columns, points), f32),
        compiler_params=pltpu.CompilerParams(vmem_limit_bytes=24 * 1024 * 1024),
        name="near",
    )(base, near_rows, in_hbm(left), in_hbm(own), in_hbm(right), blocks, far)


def doubled(pair, low):
    rank = pair.shape[1] // 2
    swapped = jnp.concatenate([pair[:, rank:], pair[:, :rank]], axis=1)
    return jnp.where(low, pair, swapped), jnp.where(low, swapped, pair)


def translated(acc, sources, table, lists, ops, base, at, low):
    for e in range(0, len(at), 4):
        picked = [sources[lists[at[e + i]] - base] for i in range(4)]
        lhs = jnp.concatenate(
            [jnp.where(low, picked[0], picked[1]), jnp.where(low, picked[2], picked[3])], axis=1
        )
        parts = [table[ops[at[e + i]]] for i in range(4)]
        rank = acc.shape[1]
        if parts[0].shape[0] < rank:
            parts = [half for t in parts for half in (t[:, :rank], t[:, rank:])]
        rhs = jnp.concatenate(parts, axis=0)
        acc = acc + mm(lhs, rhs)
    return acc


def far_kernel(
    base, list0, op0, list1, op1,
    left, own, right, leaf_ops, parent_ops, blocks, chain, parent, child, basis, *rest,
):
    siblings = rest[:-9]
    out, fetched, halo, leaf_sources, parent_sources, parent_locals, leaf_table, parent_table, sems = rest[-9:]
    leaves = basis.shape[0]
    parents = parent.shape[0]
    columns = own.shape[1]
    rank = own.shape[2] // 2
    low = lax.broadcasted_iota(jnp.int32, (columns, 2 * rank), 1) < rank
    copies = [
        pltpu.make_async_copy(source, target, sems.at[i])
        for i, (source, target) in enumerate(
            [
                (own, halo.at[1]),
                (left, halo.at[0]),
                (right, halo.at[2]),
                (parent_ops, parent_table),
                (leaf_ops, leaf_table),
                (blocks, fetched),
            ]
        )
    ]
    for copy in copies[:5]:
        copy.start()
    field = mm(siblings[0][...], chain[0], precision=highest)
    for j in range(1, len(siblings)):
        field = field + mm(siblings[j][...], chain[j], precision=highest)
    box_local = field.astype(bf16)
    for copy, i in zip(copies, (1, 0, 2)):
        copy.wait()
        for n in range(leaves // 2):
            a, b = doubled(halo[i, n], low)
            leaf_sources[i * leaves + 2 * n] = a
            leaf_sources[i * leaves + 2 * n + 1] = b
        for n in range(parents // 2):
            a, b = doubled(halo[i, leaves // 2 + n], low)
            parent_sources[i * parents + 2 * n] = a
            parent_sources[i * parents + 2 * n + 1] = b
    copies[3].wait()
    accs = [
        translated(
            mm(box_local, parent[q], NT), parent_sources, parent_table, list1, op1, base[1],
            [(q, e) for e in range(list1.shape[1])], low,
        )
        for q in range(parents)
    ]
    for q, acc in enumerate(accs):
        parent_locals[q] = acc.astype(bf16)
    copies[4].wait()
    copies[5].start()

    def one_parent(q, _):
        parent_local = parent_locals[q]
        accs = [
            translated(
                mm(parent_local, child[q * 8 + c], NT), leaf_sources, leaf_table, list0, op0, base[0],
                [(e, q * 8 + c) for e in range(list0.shape[0])], low,
            )
            for c in range(8)
        ]
        results = [mm(acc.astype(bf16), basis[q * 8 + c]) for c, acc in enumerate(accs)]
        for c, acc in enumerate(results):
            out[q * 8 + c] = acc
        return 0

    lax.fori_loop(0, parents, one_parent, 0)
    copies[5].wait()


def far_call(base, list0, op0, list1, op1, left, own, right, leaf_ops, parent_ops, blocks, siblings, chain, parent, child, basis):
    leaves, rank, points = basis.shape
    parents = parent.shape[0]
    columns = own.shape[1]
    return pl.pallas_call(
        far_kernel,
        in_specs=[SMEM] * 5 + [HBM] * 6 + [VMEM] * (4 + len(siblings)),
        out_specs=[VMEM, VMEM],
        scratch_shapes=[
            pltpu.VMEM((3,) + own.shape, bf16),
            pltpu.VMEM((3 * leaves, columns, 2 * rank), bf16),
            pltpu.VMEM((3 * parents, columns, 2 * rank), bf16),
            pltpu.VMEM((parents, columns, rank), bf16),
            pltpu.VMEM(leaf_ops.shape, bf16),
            pltpu.VMEM(parent_ops.shape, bf16),
            pltpu.SemaphoreType.DMA((6,)),
        ],
        out_shape=[jax.ShapeDtypeStruct((leaves, columns, points), f32), pltpu.VMEM(blocks.shape, bf16)],
        compiler_params=pltpu.CompilerParams(vmem_limit_bytes=24 * 1024 * 1024),
        name="far",
    )(
        base, list0, op0, list1, op1,
        *[in_hbm(x) for x in (left, own, right, leaf_ops, parent_ops, blocks)],
        chain, parent, child, basis, *siblings,
    )


def to_right(block):
    count = lax.axis_size(AXES)
    return lax.ppermute(block, AXES, [(i, i + 1) for i in range(count - 1)])


def to_left(block):
    count = lax.axis_size(AXES)
    return lax.ppermute(block, AXES, [(i + 1, i) for i in range(count - 1)])


def from_partner(block, apart):
    count = lax.axis_size(AXES)
    return lax.ppermute(block, AXES, [(i, i ^ (1 << apart)) for i in range(count)])


def after(x, *arrived):
    for y in arrived:
        x = x + jnp.minimum(jnp.abs(y[0, : x.shape[0], : x.shape[1]].astype(f32)), 0.0)
    return x


def local(
    charges, near_blocks, near_list, leaf_basis, child_transfer, parent_transfer, m2l_ops,
    far_list0, far_op0, far_list1, far_op1, top_transfer, top_couple,
):
    leaves = charges.shape[0]
    parents = parent_transfer.shape[0]
    device = lax.axis_index(AXES)
    base = jnp.stack([(device - 1) * leaves, (device - 1) * parents]).astype(jnp.int32)
    height = lax.axis_size(AXES).bit_length() - 1
    tie = lax.optimization_barrier
    charges_left = to_right(charges)
    send, total = moments_call(charges, leaf_basis, child_transfer, parent_transfer)
    siblings = []
    for level in range(height):
        if level == 1:
            total, ops = tie((total, m2l_ops))
            parent_ops, token = table_call(ops, 1, True, (), 1)
        if level == 2:
            total = after(total, charges_left)
        if level == 4:
            total, send, ops = tie((total, send, m2l_ops))
            moments_left = to_right(send)
            moments_right = to_left(send)
            leaf_ops, chain = table_call(ops, 0, False, (top_transfer, top_couple), height)
        partner = from_partner(total, level)
        if level == 1:
            partner = after(partner, token)
        if level == 4:
            partner, chain = tie((partner, chain))
        if level == height - 1:
            partner, charges, moments_left, moments_right = tie(
                (partner, charges, moments_left, moments_right)
            )
            charges_right = to_left(charges)
        siblings.append(partner)
        total = total + partner
    far, blocks = far_call(
        base, far_list0.T, far_op0.T, far_list1, far_op1,
        moments_left, send, moments_right, leaf_ops, parent_ops, near_blocks, siblings,
        chain, parent_transfer, child_transfer, leaf_basis,
    )
    return near_call(base, near_list.T, charges_left, charges, charges_right, blocks, far)


def solution(mesh):
    split = P(AXES)
    placed = (split,) * 6 + (P(),) + (split,) * 4 + (P(), P())
    return jax.shard_map(local, mesh=mesh, in_specs=placed, out_specs=split, check_vma=False)
```
